32 devices in a mesh: row: 4 (over y, x), col: 8 (over z, core).
Axes of the slice: x: 2, y: 2, z: 4, core: 2. Of those that a mesh axis runs over, the one named last changes fastest.
Arguments:
- vectors: float32 [32768, 128], P(('row', 'col')), may hold values from -6 to 6
- diagonal: float32 [32768], P(('row', 'col')), may hold values from 0.25 to 4
- source_basis: float32 [128, 256, 64], P(('row', 'col')), may hold values from -0.375 to 0.375
- transfer: float32 [7, 128, 64, 128], P(None, ('row', 'col')), may hold values from -0.5 to 0.5
- target_basis: float32 [128, 256, 64], P(('row', 'col')), may hold values from -0.75 to 0.75
Outputs:
- forward_image: float32 [32768, 128], P(('row', 'col'))
- adjoint: float32 [32768, 128], P(('row', 'col'))
The draws below stay inside these ranges and needn't reach their ends.
All inputs are finite; a program needn't handle non-finite values.
Results may differ from the reference program's by a relative error of at most 0.00017.
Values sent between devices are 32-bit elements; how exact they have to be, the bound alone decides.
No kernel may reach another device: no remote copies, remote signals or barrier semaphores. Data moves between devices by JAX's collectives and lax.ppermute only.
A program may use at most 64 MiB of HBM per device.

```python
import math
import jax
import jax.numpy as jnp
from jax import lax

LEAF = 256
RANK = 64
VECS = 128
LEAVES = 128
ROWS = 32768
LEVELS = 7


def shard_levels(own_key, shape, split, low, top_value):
    def one(position, blocks):
        steps = jax.random.uniform(jax.random.fold_in(jax.random.fold_in(own_key, 6), position), (blocks,), jnp.float32, low / len(split), top_value / len(split))
        return jnp.repeat(jnp.exp(steps), shape[position] // blocks).reshape((-1,) + (1,) * (len(shape) - position - 1))

    level = one(*split[0])
    for cut in split[1:]:
        level = level * one(*cut)
    return level


def scatter_about(own_key, dims, width, limit, cuts=(), kind=jnp.bfloat16):
    loudness = shard_levels(own_key, dims, cuts, -0.22, 0.18) if cuts else 1.0
    drawn = jax.random.normal(own_key, dims, jnp.float32) * width * loudness
    return jnp.minimum(jnp.maximum(drawn, -limit), limit).astype(kind)


def setup_inputs(seed: int = 0) -> dict:
    key_list = jax.random.split(jax.random.key(seed), 6)
    vectors = scatter_about(key_list[0], (ROWS, VECS), 1.0, 6.0, ((0, 32),), jnp.float32)
    diagonal = jnp.clip(jnp.exp(math.log(4.0) - 2.7725887 * jax.random.uniform(key_list[1], (ROWS,), jnp.float32) ** shard_levels(key_list[1], (ROWS,), ((0, 32),), -0.2, 0.2)), 0.25, 4.0)
    source_basis = scatter_about(key_list[2], (LEAVES, LEAF, RANK), LEAF ** -0.5, 0.375, ((0, 32),), jnp.float32)
    transfer = scatter_about(key_list[3], (LEVELS, LEAVES, RANK, 2 * RANK), (2 * RANK) ** -0.5, 0.5, ((1, 32),), jnp.float32)
    target_basis = scatter_about(key_list[4], (LEAVES, LEAF, RANK), RANK ** -0.5, 0.75, ((0, 32),), jnp.float32)
    return {"vectors": vectors, "diagonal": diagonal, "source_basis": source_basis, "transfer": transfer, "target_basis": target_basis}


def forward_level(coeffs, blocks, level_index):
    node_count = coeffs.shape[0]
    low_span = 2 ** level_index
    high_span = node_count // (2 * low_span)
    parted = coeffs.reshape(high_span, 2, low_span, RANK, coeffs.shape[-1])
    stacked = jnp.concatenate([parted[:, 0], parted[:, 1]], axis=2)
    shaped = blocks.reshape(high_span, 2, low_span, RANK, 2 * RANK)
    updated = jnp.einsum("aebij,abjv->aebiv", shaped, stacked, precision=lax.Precision.HIGHEST)
    return updated.reshape(node_count, RANK, coeffs.shape[-1])


def reverse_level(coeffs, blocks, level_index):
    node_count = coeffs.shape[0]
    low_span = 2 ** level_index
    high_span = node_count // (2 * low_span)
    parted = coeffs.reshape(high_span, 2, low_span, RANK, coeffs.shape[-1])
    shaped = blocks.reshape(high_span, 2, low_span, RANK, 2 * RANK)
    product = jnp.einsum("aebij,aebiv->abjv", shaped, parted, precision=lax.Precision.HIGHEST)
    halves = product.reshape(high_span, low_span, 2, RANK, coeffs.shape[-1]).transpose(0, 2, 1, 3, 4)
    return halves.reshape(node_count, RANK, coeffs.shape[-1])


def reverse_order(leafwise):
    rest_shape = leafwise.shape[1:]
    bitwise = leafwise.reshape((2,) * LEVELS + rest_shape)
    axes_order = list(range(LEVELS - 1, -1, -1)) + list(range(LEVELS, LEVELS + len(rest_shape)))
    return jnp.transpose(bitwise, axes_order).reshape(leafwise.shape)


def reference(vectors, diagonal, source_basis, transfer, target_basis):
    leaf_rows = vectors.reshape(LEAVES, LEAF, VECS)
    coeffs = jnp.einsum("ksr,ksv->krv", source_basis, leaf_rows, precision=lax.Precision.HIGHEST)
    for level_index in range(LEVELS):
        coeffs = forward_level(coeffs, transfer[level_index], level_index)
    leaf_image = jnp.einsum("ksr,krv->ksv", target_basis, coeffs, precision=lax.Precision.HIGHEST)
    ordered = reverse_order(leaf_image)
    forward_image = ordered.reshape(ROWS, VECS)
    weighted = diagonal.reshape(LEAVES, LEAF)[:, :, None] * ordered
    weighted_leaf = reverse_order(weighted)
    adjoint_coeffs = jnp.einsum("ksr,ksv->krv", target_basis, weighted_leaf, precision=lax.Precision.HIGHEST)
    for level_index in range(LEVELS - 1, -1, -1):
        adjoint_coeffs = reverse_level(adjoint_coeffs, transfer[level_index], level_index)
    adjoint = jnp.einsum("ksr,krv->ksv", source_basis, adjoint_coeffs, precision=lax.Precision.HIGHEST)
    return forward_image, adjoint.reshape(ROWS, VECS)
```

```python
import jax
import jax.numpy as jnp
from jax import lax
from jax.sharding import PartitionSpec as P

HIGHEST = lax.Precision.HIGHEST
BOTH = ("row", "col")


def reverse_bits(value, bits):
    out = 0
    for i in range(bits):
        out = out | ((value >> i) & 1) << (bits - 1 - i)
    return out


def pair_exchange(block, axis, bit):
    count = lax.axis_size(axis)
    return lax.ppermute(block, axis, [(i, i ^ (1 << bit)) for i in range(count)])


class Reversal:
    def __init__(self, local_bits):
        self.rows = lax.axis_size("row")
        self.cols = lax.axis_size("col")
        self.bits = (self.rows * self.cols).bit_length() - 1
        self.local_bits = local_bits
        self.count = 2**local_bits
        place = lax.axis_index("row") * self.cols + lax.axis_index("col")
        self.top = place >> (self.bits - local_bits)

    def route(self, k):
        low = self.bits - self.local_bits
        return [
            (d, ((d >> low) ^ k) << low | reverse_bits(d & (2**low - 1), low))
            for d in range(2**self.bits)
        ]

    def slot(self, k):
        return reverse_bits(self.top ^ k, self.local_bits)

    def send(self, blocks, k):
        picked = lax.dynamic_index_in_dim(blocks, self.slot(k), 0, keepdims=False)
        return lax.ppermute(picked, BOTH, self.route(k))

    def place(self, arrived):
        out = jnp.zeros((self.count,) + arrived[0].shape, arrived[0].dtype)
        for k, block in enumerate(arrived):
            out = lax.dynamic_update_index_in_dim(out, block, self.slot(k), 0)
        return out


def local_forward(coeffs, blocks, level):
    count, rank, vecs = coeffs.shape
    low = 2**level
    parted = coeffs.reshape(count // (2 * low), 2, low, rank, vecs)
    stacked = jnp.concatenate([parted[:, 0], parted[:, 1]], axis=2)
    shaped = blocks.reshape(count // (2 * low), 2, low, rank, 2 * rank)
    out = jnp.einsum("aebij,abjv->aebiv", shaped, stacked, precision=HIGHEST)
    return out.reshape(count, rank, vecs)


def local_reverse(coeffs, blocks, level):
    count, rank, vecs = coeffs.shape
    low = 2**level
    parted = coeffs.reshape(count // (2 * low), 2, low, rank, vecs)
    shaped = blocks.reshape(count // (2 * low), 2, low, rank, 2 * rank)
    out = jnp.einsum("aebij,aebiv->abjv", shaped, parted, precision=HIGHEST)
    halves = out.reshape(count // (2 * low), low, 2, rank, vecs).transpose(0, 2, 1, 3, 4)
    return halves.reshape(count, rank, vecs)


def body(vectors, diagonal, source_basis, transfer, target_basis):
    leaves, leaf, rank = source_basis.shape
    vecs = vectors.shape[-1]
    local_bits = leaves.bit_length() - 1
    col_bits = lax.axis_size("col").bit_length() - 1
    row_bits = lax.axis_size("row").bit_length() - 1
    steps = [("col", bit) for bit in range(col_bits)] + [("row", bit) for bit in range(row_bits)]
    uppers = [lax.axis_index(axis) >> bit & 1 == 1 for axis, bit in steps]
    levels = [transfer[local_bits + i] for i in range(len(steps))]
    reversal = Reversal(local_bits)

    diag_blocks = diagonal.reshape(leaves, leaf)
    weights = reversal.place([reversal.send(diag_blocks, k) for k in range(leaves)])
    gram = jnp.einsum(
        "ksr,kst->krt", target_basis * weights[:, :, None], target_basis, precision=HIGHEST
    )
    top = levels[-1]
    fold = jnp.einsum("krt,ktj->krj", gram, top, precision=HIGHEST)
    fold = jnp.einsum("kri,krj->kij", top, fold, precision=HIGHEST)
    kept = jnp.where(uppers[-1], fold[:, rank:], fold[:, :rank])
    sent = jnp.where(uppers[-1], fold[:, :rank], fold[:, rank:])
    fold = kept + pair_exchange(sent, *steps[-1])

    coeffs = jnp.einsum(
        "ksr,ksv->krv", source_basis, vectors.reshape(leaves, leaf, vecs), precision=HIGHEST
    )
    for level in range(local_bits):
        coeffs = local_forward(coeffs, transfer[level], level)

    def stacked_pair(coeffs, i):
        partner = pair_exchange(coeffs, *steps[i])
        lower = jnp.where(uppers[i], partner, coeffs)
        upper = jnp.where(uppers[i], coeffs, partner)
        return jnp.concatenate([lower, upper], axis=1)

    for i in range(len(steps) - 1):
        stacked = stacked_pair(coeffs, i)
        coeffs = jnp.einsum("nij,njv->niv", levels[i], stacked, precision=HIGHEST)
    stacked = stacked_pair(coeffs, len(steps) - 1)
    back = jnp.einsum("nij,njv->niv", fold, stacked, precision=HIGHEST)
    coeffs = jnp.einsum("nij,njv->niv", top, stacked, precision=HIGHEST)

    image = jnp.einsum("ksr,krv->ksv", target_basis, coeffs, precision=HIGHEST)
    forward_image = reversal.place([reversal.send(image, k) for k in range(leaves)])

    for i in range(len(steps) - 2, -1, -1):
        product = jnp.einsum("nij,niv->njv", levels[i], back, precision=HIGHEST)
        kept = jnp.where(uppers[i], product[:, rank:], product[:, :rank])
        sent = jnp.where(uppers[i], product[:, :rank], product[:, rank:])
        back = kept + pair_exchange(sent, *steps[i])
    for level in range(local_bits - 1, -1, -1):
        back = local_reverse(back, transfer[level], level)
    adjoint = jnp.einsum("ksr,krv->ksv", source_basis, back, precision=HIGHEST)
    return forward_image.reshape(leaves * leaf, vecs), adjoint.reshape(leaves * leaf, vecs)


def solution(mesh):
    placed = (
        P(BOTH, None),
        P(BOTH),
        P(BOTH, None, None),
        P(None, BOTH, None, None),
        P(BOTH, None, None),
    )
    return jax.shard_map(
        body, mesh=mesh, in_specs=placed, out_specs=(P(BOTH, None), P(BOTH, None)), check_vma=False
    )
```

```python
import jax
import jax.numpy as jnp
from jax import lax
from jax.sharding import PartitionSpec as P

HIGHEST = lax.Precision.HIGHEST
BOTH = ("row", "col")


def reverse_bits(value, bits):
    out = 0
    for i in range(bits):
        out = out | ((value >> i) & 1) << (bits - 1 - i)
    return out


class Places:
    def __init__(self, slot_bits):
        self.devices = lax.axis_size("row") * lax.axis_size("col")
        self.slot_bits = slot_bits
        self.low_bits = self.devices.bit_length() - 1 - slot_bits
        self.place = lax.axis_index("row") * lax.axis_size("col") + lax.axis_index("col")
        self.top = self.place >> self.low_bits

    def permute(self, block, route):
        return lax.ppermute(block, BOTH, [(d, route(d)) for d in range(self.devices)])

    def partner(self, block, bit):
        return self.permute(block, lambda d: d ^ (1 << bit))

    def upper(self, bit):
        return (self.place >> bit) & 1 == 1

    def reverse_low(self, block):
        low = self.low_bits
        return self.permute(
            block, lambda d: (d >> low) << low | reverse_bits(d & (2**low - 1), low)
        )

    def slot(self, k):
        return reverse_bits(self.top ^ k, self.slot_bits)

    def swap(self, blocks):
        out = blocks
        for k in range(1, 2**self.slot_bits):
            picked = lax.dynamic_index_in_dim(blocks, self.slot(k), 0, keepdims=False)
            moved = self.permute(picked, lambda d: d ^ (k << self.low_bits))
            out = lax.dynamic_update_index_in_dim(out, moved, self.slot(k), 0)
        return out


def local_forward(coeffs, blocks, bit):
    count, rank, vecs = coeffs.shape
    low = 2**bit
    parted = coeffs.reshape(count // (2 * low), 2, low, rank, vecs)
    stacked = jnp.concatenate([parted[:, 0], parted[:, 1]], axis=2)
    shaped = blocks.reshape(count // (2 * low), 2, low, rank, 2 * rank)
    out = jnp.einsum("aebij,abjv->aebiv", shaped, stacked, precision=HIGHEST)
    return out.reshape(count, rank, vecs)


def local_reverse(coeffs, blocks, bit):
    count, rank, vecs = coeffs.shape
    low = 2**bit
    parted = coeffs.reshape(count // (2 * low), 2, low, rank, vecs)
    shaped = blocks.reshape(count // (2 * low), 2, low, rank, 2 * rank)
    out = jnp.einsum("aebij,aebiv->abjv", shaped, parted, precision=HIGHEST)
    halves = out.reshape(count // (2 * low), low, 2, rank, vecs).transpose(0, 2, 1, 3, 4)
    return halves.reshape(count, rank, vecs)


def body(vectors, diagonal, source_basis, transfer, target_basis):
    leaves, leaf, rank = source_basis.shape
    vecs = vectors.shape[-1]
    slot_bits = leaves.bit_length() - 1
    places = Places(slot_bits)
    pair_bits = range(places.low_bits)
    pair_levels = [transfer[slot_bits + bit] for bit in pair_bits]

    basis_t = jnp.swapaxes(target_basis, 1, 2)
    tops = [transfer[slot_bits + places.low_bits + j] for j in range(slot_bits)]
    moving = jnp.concatenate(
        [t.reshape(leaves, -1) for t in tops] + [basis_t.reshape(leaves, -1)], axis=1
    ).reshape(leaves, -1, 128)
    moved = places.swap(moving).reshape(leaves, -1)
    size = rank * 2 * rank
    tops = [
        moved[:, j * size : (j + 1) * size].reshape(leaves, rank, 2 * rank)
        for j in range(slot_bits)
    ]
    basis_t = moved[:, slot_bits * size :].reshape(leaves, rank, leaf)
    weights = places.reverse_low(diagonal).reshape(leaves, leaf)
    gram = jnp.einsum(
        "krs,kts->krt", basis_t * weights[:, None, :], basis_t, precision=HIGHEST
    )
    image_basis_t = places.reverse_low(basis_t)
    wide = jnp.eye(leaves * rank, dtype=jnp.float32).reshape(leaves, rank, leaves * rank)
    for j in range(slot_bits):
        wide = local_forward(wide, tops[j], slot_bits - 1 - j)
    middle = jnp.einsum("krt,kti->kri", gram, wide, precision=HIGHEST)
    middle = jnp.einsum("krj,kri->ji", wide, middle, precision=HIGHEST)

    coeffs = jnp.einsum(
        "ksr,ksv->krv", source_basis, vectors.reshape(leaves, leaf, vecs), precision=HIGHEST
    )
    for level in range(slot_bits):
        coeffs = local_forward(coeffs, transfer[level], level)
    for bit in pair_bits:
        other = places.partner(coeffs, bit)
        lower = jnp.where(places.upper(bit), other, coeffs)
        upper = jnp.where(places.upper(bit), coeffs, other)
        stacked = jnp.concatenate([lower, upper], axis=1)
        coeffs = jnp.einsum("nij,njv->niv", pair_levels[bit], stacked, precision=HIGHEST)

    stacked = places.swap(coeffs).reshape(leaves * rank, vecs)
    back = jnp.einsum("ij,jv->iv", middle, stacked, precision=HIGHEST)
    back = places.swap(back.reshape(leaves, rank, vecs))
    coeffs = jnp.einsum("krj,jv->krv", wide, stacked, precision=HIGHEST)
    image_coeffs = places.reverse_low(coeffs)
    forward_image = jnp.einsum(
        "krs,krv->ksv", image_basis_t, image_coeffs, precision=HIGHEST
    )

    for bit in reversed(pair_bits):
        product = jnp.einsum("nij,niv->njv", pair_levels[bit], back, precision=HIGHEST)
        kept = jnp.where(places.upper(bit), product[:, rank:], product[:, :rank])
        sent = jnp.where(places.upper(bit), product[:, :rank], product[:, rank:])
        back = kept + places.partner(sent, bit)
    for level in range(slot_bits - 1, -1, -1):
        back = local_reverse(back, transfer[level], level)
    adjoint = jnp.einsum("ksr,krv->ksv", source_basis, back, precision=HIGHEST)
    return forward_image.reshape(leaves * leaf, vecs), adjoint.reshape(leaves * leaf, vecs)


def solution(mesh):
    placed = (
        P(BOTH, None),
        P(BOTH),
        P(BOTH, None, None),
        P(None, BOTH, None, None),
        P(BOTH, None, None),
    )
    return jax.shard_map(
        body, mesh=mesh, in_specs=placed, out_specs=(P(BOTH, None), P(BOTH, None)), check_vma=False
    )
```

```python
import jax
import jax.numpy as jnp
from jax import lax
from jax.sharding import PartitionSpec as P


PRECISION = lax.Precision.HIGH
BOTH = ("row", "col")


def reverse_bits(value, bits):
    out = 0
    for i in range(bits):
        out = out | ((value >> i) & 1) << (bits - 1 - i)
    return out


class Places:
    def __init__(self, slot_bits):
        self.devices = lax.axis_size("row") * lax.axis_size("col")
        self.slot_bits = slot_bits
        self.low_bits = self.devices.bit_length() - 1 - slot_bits
        self.place = lax.axis_index("row") * lax.axis_size("col") + lax.axis_index("col")
        self.top = self.place >> self.low_bits

    def permute(self, block, route):
        return lax.ppermute(block, BOTH, [(d, route(d)) for d in range(self.devices)])

    def partner(self, block, bit):
        return self.permute(block, lambda d: d ^ (1 << bit))

    def upper(self, bit):
        return (self.place >> bit) & 1 == 1

    def reverse_low(self, block):
        low = self.low_bits
        return self.permute(
            block, lambda d: (d >> low) << low | reverse_bits(d & (2**low - 1), low)
        )

    def slot(self, k):
        return reverse_bits(self.top ^ k, self.slot_bits)

    def across(self, block, k):
        return self.permute(block, lambda d: d ^ (k << self.low_bits))

    def gather(self, blocks):
        picked = [
            lax.dynamic_index_in_dim(blocks, self.slot(k), 0, keepdims=False)
            for k in range(2**self.slot_bits)
        ]
        return [b if k == 0 else self.across(b, k) for k, b in enumerate(picked)]

    def scatter(self, blocks):
        arrived = [b if k == 0 else self.across(b, k) for k, b in enumerate(blocks)]
        return self.in_order(arrived)

    def in_order(self, arrived):
        out = jnp.zeros((len(arrived),) + arrived[0].shape, arrived[0].dtype)
        for k, block in enumerate(arrived):
            out = lax.dynamic_update_index_in_dim(out, block, self.slot(k), 0)
        return out


def local_forward(coeffs, blocks, bit):
    count, rank, vecs = coeffs.shape
    low = 2**bit
    parted = coeffs.reshape(count // (2 * low), 2, low, rank, vecs)
    stacked = jnp.concatenate([parted[:, 0], parted[:, 1]], axis=2)
    shaped = blocks.reshape(count // (2 * low), 2, low, rank, 2 * rank)
    out = jnp.einsum("aebij,abjv->aebiv", shaped, stacked, precision=PRECISION)
    return out.reshape(count, rank, vecs)


def local_reverse(coeffs, blocks, bit):
    count, rank, vecs = coeffs.shape
    low = 2**bit
    parted = coeffs.reshape(count // (2 * low), 2, low, rank, vecs)
    shaped = blocks.reshape(count // (2 * low), 2, low, rank, 2 * rank)
    out = jnp.einsum("aebij,aebiv->abjv", shaped, parted, precision=PRECISION)
    halves = out.reshape(count // (2 * low), low, 2, rank, vecs).transpose(0, 2, 1, 3, 4)
    return halves.reshape(count, rank, vecs)


def body(vectors, diagonal, source_basis, transfer, target_basis):
    leaves, leaf, rank = source_basis.shape
    vecs = vectors.shape[-1]
    slot_bits = leaves.bit_length() - 1
    places = Places(slot_bits)
    pair_bits = range(places.low_bits)
    pair_levels = [transfer[slot_bits + bit] for bit in pair_bits]

    basis_t = jnp.swapaxes(target_basis, 1, 2)
    tops = [transfer[slot_bits + places.low_bits + j] for j in range(slot_bits)]
    halves = [basis_t[:, :, j : j + vecs] for j in range(0, leaf, vecs)]
    moving = jnp.concatenate(tops + halves, axis=1)
    moved = places.gather(moving)
    moved = places.in_order(moved)
    parts = [moved[:, j : j + rank] for j in range(0, moved.shape[1], rank)]
    tops = parts[:slot_bits]
    basis_t = jnp.concatenate(parts[slot_bits:], axis=2)
    weights = places.reverse_low(diagonal).reshape(leaves, leaf)
    order = jnp.stack([places.slot(k) for k in range(leaves)])
    chosen = jnp.arange(leaves)[:, None] == order[None, :]
    wide = chosen[:, None, :, None] & jnp.eye(rank, dtype=bool)[None, :, None, :]
    wide = wide.astype(jnp.float32).reshape(leaves, rank, leaves * rank)
    gram = jnp.einsum("krs,kts->krt", basis_t * weights[:, None, :], basis_t, precision=PRECISION)
    for j in range(slot_bits):
        wide = local_forward(wide, tops[j], slot_bits - 1 - j)
    middle = jnp.einsum("krt,kti->kri", gram, wide, precision=PRECISION)
    middle = jnp.einsum("krj,kri->ji", wide, middle, precision=PRECISION)

    coeffs = jnp.einsum(
        "ksr,ksv->krv", source_basis, vectors.reshape(leaves, leaf, vecs), precision=PRECISION
    )
    for level in range(slot_bits):
        coeffs = local_forward(coeffs, transfer[level], level)
    for bit in pair_bits:
        other = places.partner(coeffs, bit)
        lower = jnp.where(places.upper(bit), other, coeffs)
        upper = jnp.where(places.upper(bit), coeffs, other)
        stacked = jnp.concatenate([lower, upper], axis=1)
        coeffs = jnp.einsum("nij,njv->niv", pair_levels[bit], stacked, precision=PRECISION)

    stacked = jnp.concatenate(places.gather(coeffs), axis=0)
    back = jnp.einsum("ij,jv->iv", middle, stacked, precision=PRECISION)
    back = places.scatter(list(back.reshape(leaves, rank, vecs)))
    coeffs = jnp.einsum("krj,jv->krv", wide, stacked, precision=PRECISION)
    forward_image = jnp.einsum("krs,krv->ksv", basis_t, coeffs, precision=PRECISION)
    forward_image = places.reverse_low(forward_image)

    for bit in reversed(pair_bits):
        product = jnp.einsum("nij,niv->njv", pair_levels[bit], back, precision=PRECISION)
        kept = jnp.where(places.upper(bit), product[:, rank:], product[:, :rank])
        sent = jnp.where(places.upper(bit), product[:, :rank], product[:, rank:])
        back = kept + places.partner(sent, bit)
    for level in range(slot_bits - 1, -1, -1):
        back = local_reverse(back, transfer[level], level)
    adjoint = jnp.einsum("ksr,krv->ksv", source_basis, back, precision=PRECISION)
    return forward_image.reshape(leaves * leaf, vecs), adjoint.reshape(leaves * leaf, vecs)


def solution(mesh):
    placed = (
        P(BOTH, None),
        P(BOTH),
        P(BOTH, None, None),
        P(None, BOTH, None, None),
        P(BOTH, None, None),
    )

    return jax.shard_map(
        body, mesh=mesh, in_specs=placed, out_specs=(P(BOTH, None), P(BOTH, None)), check_vma=False
    )
```

```python
import jax
import jax.numpy as jnp
from jax import lax
from jax.sharding import PartitionSpec as P


PRECISION = lax.Precision.HIGHEST
BOTH = ("row", "col")


def reverse_bits(value, bits):
    out = 0
    for i in range(bits):
        out = out | ((value >> i) & 1) << (bits - 1 - i)
    return out


class Places:
    def __init__(self, slot_bits):
        self.devices = lax.axis_size("row") * lax.axis_size("col")
        self.slot_bits = slot_bits
        self.low_bits = self.devices.bit_length() - 1 - slot_bits
        self.place = lax.axis_index("row") * lax.axis_size("col") + lax.axis_index("col")
        self.top = self.place >> self.low_bits

    def permute(self, block, route):
        return lax.ppermute(block, BOTH, [(d, route(d)) for d in range(self.devices)])

    def partner(self, block, bit):
        return self.permute(block, lambda d: d ^ (1 << bit))

    def upper(self, bit):
        return (self.place >> bit) & 1 == 1

    def reverse_low(self, block):
        low = self.low_bits
        return self.permute(
            block, lambda d: (d >> low) << low | reverse_bits(d & (2**low - 1), low)
        )

    def slot(self, k):
        return reverse_bits(self.top ^ k, self.slot_bits)

    def across(self, block, k):
        return self.permute(block, lambda d: d ^ (k << self.low_bits))

    def gather(self, blocks):
        picked = [
            lax.dynamic_index_in_dim(blocks, self.slot(k), 0, keepdims=False)
            for k in range(2**self.slot_bits)
        ]
        return [b if k == 0 else self.across(b, k) for k, b in enumerate(picked)]

    def scatter(self, blocks):
        arrived = [b if k == 0 else self.across(b, k) for k, b in enumerate(blocks)]
        return self.in_order(arrived)

    def in_order(self, arrived):
        out = jnp.zeros((len(arrived),) + arrived[0].shape, arrived[0].dtype)
        for k, block in enumerate(arrived):
            out = lax.dynamic_update_index_in_dim(out, block, self.slot(k), 0)
        return out


def local_forward(coeffs, blocks, bit):
    count, rank, vecs = coeffs.shape
    low = 2**bit
    parted = coeffs.reshape(count // (2 * low), 2, low, rank, vecs)
    stacked = jnp.concatenate([parted[:, 0], parted[:, 1]], axis=2)
    shaped = blocks.reshape(count // (2 * low), 2, low, rank, 2 * rank)
    out = jnp.einsum("aebij,abjv->aebiv", shaped, stacked, precision=PRECISION)
    return out.reshape(count, rank, vecs)


def local_reverse(coeffs, blocks, bit):
    count, rank, vecs = coeffs.shape
    low = 2**bit
    parted = coeffs.reshape(count // (2 * low), 2, low, rank, vecs)
    shaped = blocks.reshape(count // (2 * low), 2, low, rank, 2 * rank)
    out = jnp.einsum("aebij,aebiv->abjv", shaped, parted, precision=PRECISION)
    halves = out.reshape(count // (2 * low), low, 2, rank, vecs).transpose(0, 2, 1, 3, 4)
    return halves.reshape(count, rank, vecs)


def body(vectors, diagonal, source_basis, transfer, target_basis):
    leaves, leaf, rank = source_basis.shape
    vecs = vectors.shape[-1]
    slot_bits = leaves.bit_length() - 1
    places = Places(slot_bits)
    pair_bits = range(places.low_bits)
    pair_levels = [transfer[slot_bits + bit] for bit in pair_bits]

    basis_t = jnp.swapaxes(target_basis, 1, 2)
    tops = [transfer[slot_bits + places.low_bits + j] for j in range(slot_bits)]
    halves = [basis_t[:, :, j : j + vecs] for j in range(0, leaf, vecs)]
    moving = jnp.concatenate(tops + halves, axis=1)
    moved = places.gather(moving)
    moved = places.in_order(moved)
    parts = [moved[:, j : j + rank] for j in range(0, moved.shape[1], rank)]
    tops = parts[:slot_bits]
    basis_t = jnp.concatenate(parts[slot_bits:], axis=2)
    weights = places.reverse_low(diagonal).reshape(leaves, leaf)
    order = jnp.stack([places.slot(k) for k in range(leaves)])
    chosen = jnp.arange(leaves)[:, None] == order[None, :]
    wide = chosen[:, None, :, None] & jnp.eye(rank, dtype=bool)[None, :, None, :]
    wide = wide.astype(jnp.float32).reshape(leaves, rank, leaves * rank)
    gram = jnp.einsum("krs,kts->krt", basis_t * weights[:, None, :], basis_t, precision=PRECISION)
    for j in range(slot_bits):
        wide = local_forward(wide, tops[j], slot_bits - 1 - j)
    middle = jnp.einsum("krt,kti->kri", gram, wide, precision=PRECISION)
    middle = jnp.einsum("krj,kri->ji", wide, middle, precision=PRECISION)

    coeffs = jnp.einsum(
        "ksr,ksv->krv", source_basis, vectors.reshape(leaves, leaf, vecs), precision=PRECISION
    )
    for level in range(slot_bits):
        coeffs = local_forward(coeffs, transfer[level], level)
    for bit in pair_bits:
        other = places.partner(coeffs, bit)
        lower = jnp.where(places.upper(bit), other, coeffs)
        upper = jnp.where(places.upper(bit), coeffs, other)
        stacked = jnp.concatenate([lower, upper], axis=1)
        coeffs = jnp.einsum("nij,njv->niv", pair_levels[bit], stacked, precision=PRECISION)

    stacked = jnp.concatenate(places.gather(coeffs), axis=0)
    back = jnp.einsum("ij,jv->iv", middle, stacked, precision=PRECISION)
    back = places.scatter(list(back.reshape(leaves, rank, vecs)))
    coeffs = jnp.einsum("krj,jv->krv", wide, stacked, precision=PRECISION)
    image_coeffs = places.reverse_low(coeffs)
    image_basis = places.reverse_low(basis_t)
    forward_image = jnp.einsum(
        "krs,krv->ksv", image_basis, image_coeffs, precision=PRECISION
    )

    for bit in reversed(pair_bits):
        product = jnp.einsum("nij,niv->njv", pair_levels[bit], back, precision=PRECISION)
        kept = jnp.where(places.upper(bit), product[:, rank:], product[:, :rank])
        sent = jnp.where(places.upper(bit), product[:, :rank], product[:, rank:])
        back = kept + places.partner(sent, bit)
    for level in range(slot_bits - 1, -1, -1):
        back = local_reverse(back, transfer[level], level)
    adjoint = jnp.einsum("ksr,krv->ksv", source_basis, back, precision=PRECISION)
    return forward_image.reshape(leaves * leaf, vecs), adjoint.reshape(leaves * leaf, vecs)


def solution(mesh):
    placed = (
        P(BOTH, None),
        P(BOTH),
        P(BOTH, None, None),
        P(None, BOTH, None, None),
        P(BOTH, None, None),
    )

    return jax.shard_map(
        body, mesh=mesh, in_specs=placed, out_specs=(P(BOTH, None), P(BOTH, None)), check_vma=False
    )
```

```python
import functools

import jax
import jax.numpy as jnp
from jax import lax
from jax.experimental import pallas as pl
from jax.experimental.pallas import tpu as pltpu
from jax.sharding import PartitionSpec as P


SLOT_BITS = 2
SLOTS = 2**SLOT_BITS
BOTH = ("row", "col")
NN, TN, NT = ((1,), (0,)), ((0,), (0,)), ((1,), (1,))
VMEM = pl.BlockSpec(memory_space=pltpu.VMEM)
SMEM = pl.BlockSpec(memory_space=pltpu.SMEM)
ANY = pl.BlockSpec(memory_space=pl.ANY)
HBM = pl.BlockSpec(memory_space=pltpu.HBM)


def reverse_bits(value, bits):
    out = 0
    for i in range(bits):
        out = out | ((value >> i) & 1) << (bits - 1 - i)
    return out


class Places:
    def __init__(self, slot_bits):
        self.devices = lax.axis_size("row") * lax.axis_size("col")
        self.slot_bits = slot_bits
        self.low_bits = self.devices.bit_length() - 1 - slot_bits
        self.place = lax.axis_index("row") * lax.axis_size("col") + lax.axis_index("col")
        self.top = self.place >> self.low_bits

    def permute(self, block, route):
        return lax.ppermute(block, BOTH, [(d, route(d)) for d in range(self.devices)])

    def partner(self, block, bit):
        return self.permute(block, lambda d: d ^ (1 << bit))

    def reverse_low(self, block):
        low = self.low_bits
        return self.permute(
            block, lambda d: (d >> low) << low | reverse_bits(d & (2**low - 1), low)
        )

    def across(self, blocks):
        return [
            b if k == 0 else self.permute(b, lambda d: d ^ (k << self.low_bits))
            for k, b in enumerate(blocks)
        ]

    def scalars(self):
        order = [reverse_bits(self.top ^ k, self.slot_bits) for k in range(SLOTS)]
        bits = [(self.place >> bit) & 1 for bit in range(self.low_bits)]
        return jnp.stack(order + bits).astype(jnp.int32)


def split(x):
    high = x.astype(jnp.bfloat16)
    return high, (x - high.astype(jnp.float32)).astype(jnp.bfloat16)


def product(a, b, dims):
    (ah, al), (bh, bl) = split(a), split(b)

    def dot(x, y):
        return lax.dot_general(x, y, (dims, ((), ())), preferred_element_type=jnp.float32)

    return dot(ah, bh) + (dot(ah, bl) + dot(al, bh))


def call(kernel, outs, operands, specs=None, out_specs=None, scratch=(), flops=1 << 24):
    shapes = [jax.ShapeDtypeStruct(s, jnp.float32) for s in outs]
    return pl.pallas_call(
        kernel,
        out_shape=shapes,
        in_specs=specs or [VMEM] * len(operands),
        out_specs=out_specs or [VMEM] * len(outs),
        scratch_shapes=list(scratch),
        compiler_params=pltpu.CompilerParams(vmem_limit_bytes=8 << 20),
        cost_estimate=pl.CostEstimate(flops=flops, bytes_accessed=1 << 19, transcendentals=0),
    )(*operands)


def pairs(bit):
    return [(s, s | 1 << bit) for s in range(SLOTS) if not s >> bit & 1]


def head_kernel(vectors_in, basis_in, transfer_in, target_in, out, basis, transfer, target, vectors, sems):
    leaf = basis.shape[2]
    copies = []

    def fetch(source, to):
        copies.append(pltpu.make_async_copy(source, to, sems.at[len(copies)]))
        copies[-1].start()
        return copies[-1]

    slots = []
    for s in range(SLOTS):
        rows = pl.ds(s * leaf, leaf)
        slots.append(
            (fetch(basis_in.at[s], basis.at[s]), fetch(vectors_in.at[rows], vectors.at[rows]))
        )
    first = fetch(transfer_in.at[pl.ds(0, SLOT_BITS)], transfer.at[pl.ds(0, SLOT_BITS)])
    rest = pl.ds(SLOT_BITS, transfer.shape[0] - SLOT_BITS)
    later = [fetch(transfer_in.at[rest], transfer.at[rest]), fetch(target_in, target)]
    c = []
    for s in range(SLOTS):
        for copy in slots[s]:
            copy.wait()
        c.append(product(basis[s], vectors[s * leaf : (s + 1) * leaf], NN))
    first.wait()
    for level in range(SLOT_BITS):
        for low, high in pairs(level):
            both = jnp.concatenate([c[low], c[high]], axis=0)
            c[low] = product(transfer[level, low], both, NN)
            c[high] = product(transfer[level, high], both, NN)
    for s in range(SLOTS):
        out[s] = c[s]
    for copy in later:
        copy.wait()


def join(level, bit, s, meta, own, partner, transfer):
    upper = meta[SLOTS + bit] == 1
    lower_half = jnp.where(upper, partner[s], own[s])
    upper_half = jnp.where(upper, own[s], partner[s])
    return product(transfer[level, s], jnp.concatenate([lower_half, upper_half], axis=0), NN)


def pair_kernel(level, bit, meta, own, partner, transfer, out):
    for s in range(SLOTS):
        out[s] = join(level, bit, s, meta, own, partner, transfer)


def last_pair_kernel(level, bit, meta, own, partner, transfer, *outs):
    for k in range(SLOTS):
        outs[k][...] = join(level, bit, meta[k], meta, own, partner, transfer)


def pick_kernel(tops, meta, transfer, basis, *outs):
    rank, leaf = basis.shape[1:]
    width = transfer.shape[3]
    for k in range(SLOTS):
        s = meta[k]
        parts = [transfer[level, s] for level in tops]
        parts += [basis[s, :, j : j + width] for j in range(0, leaf, width)]
        for j, part in enumerate(parts):
            outs[k][j * rank : (j + 1) * rank] = part


def arrange_kernel(meta, *refs):
    moved, tops, basis = refs[:SLOTS], refs[SLOTS], refs[SLOTS + 1]
    rank, width = tops.shape[2:]
    for k in range(SLOTS):
        s = meta[k]
        for j in range(SLOT_BITS):
            tops[j, s] = moved[k][j * rank : (j + 1) * rank]
        for j in range(basis.shape[2] // width):
            row = (SLOT_BITS + j) * rank
            basis[s, :, j * width : (j + 1) * width] = moved[k][row : row + rank]


def fold_kernel(meta, tops, basis, weights, wide, middle, columns):
    rank = basis.shape[1]
    blocks = [tops[0, s] for s in range(SLOTS)]
    high = 1 << (SLOT_BITS - 1)
    sources = [[s & ~high, s | high] for s in range(SLOTS)]
    for j in range(1, SLOT_BITS):
        bit = 1 << (SLOT_BITS - 1 - j)
        old, old_sources = blocks, sources
        blocks, sources = [], []
        for s in range(SLOTS):
            halves = [
                product(tops[j, s][:, e * rank : (e + 1) * rank], old[q], NN)
                for e, q in enumerate((s & ~bit, s | bit))
            ]
            blocks.append(jnp.concatenate(halves, axis=1))
            sources.append(old_sources[s & ~bit] + old_sources[s | bit])
    for s in range(SLOTS):
        for at, source in enumerate(sources[s]):
            columns[source, s * rank : (s + 1) * rank] = blocks[s][:, at * rank : (at + 1) * rank]
    ordered = jnp.concatenate([columns[meta[k]] for k in range(SLOTS)], axis=1)
    wide[...] = ordered
    inner = []
    for s in range(SLOTS):
        gram = product(basis[s] * weights[s : s + 1, :], basis[s], NT)
        inner.append(product(gram, ordered[s * rank : (s + 1) * rank], NN))
    middle[...] = product(ordered, jnp.concatenate(inner, axis=0), TN)


def middle_kernel(middle, *refs):
    blocks, outs = refs[:SLOTS], refs[SLOTS:]
    rank = blocks[0].shape[0]
    out = product(middle[...], jnp.concatenate([b[...] for b in blocks], axis=0), NN)
    for k in range(SLOTS):
        outs[k][...] = out[k * rank : (k + 1) * rank]


def top_kernel(wide, *refs):
    blocks, out = refs[:SLOTS], refs[SLOTS]
    rank = blocks[0].shape[0]
    rows = product(wide[...], jnp.concatenate([b[...] for b in blocks], axis=0), NN)
    for s in range(SLOTS):
        out[s] = rows[s * rank : (s + 1) * rank]


def part(level, bit, s, meta, block, transfer, sent, kept):
    upper = meta[SLOTS + bit] == 1
    out = product(transfer[level, s], block, TN)
    rank = sent.shape[1]
    sent[s] = jnp.where(upper, out[:rank], out[rank:])
    kept[s] = jnp.where(upper, out[rank:], out[:rank])


def first_part_kernel(level, bit, meta, transfer, *refs):
    for k in range(SLOTS):
        part(level, bit, meta[k], meta, refs[k][...], transfer, *refs[SLOTS:])


def part_kernel(level, bit, meta, transfer, kept_in, arrived, sent, kept):
    for s in range(SLOTS):
        part(level, bit, s, meta, kept_in[s] + arrived[s], transfer, sent, kept)


def write_rows(rows, out, buffer, sems):
    copies = []
    for s in range(SLOTS):
        leaf = buffer.shape[1]
        buffer[s] = rows(s)
        copies.append(
            pltpu.make_async_copy(buffer.at[s], out.at[pl.ds(s * leaf, leaf)], sems.at[s])
        )
        copies[-1].start()
    for copy in copies:
        copy.wait()


def tail_kernel(kept, arrived, transfer, basis, out, buffer, sems):
    b = [kept[s] + arrived[s] for s in range(SLOTS)]
    rank = b[0].shape[0]
    for level in reversed(range(SLOT_BITS)):
        for low, high in pairs(level):
            blocks = jnp.concatenate([transfer[level, low], transfer[level, high]], axis=0)
            both = product(blocks, jnp.concatenate([b[low], b[high]], axis=0), TN)
            b[low], b[high] = both[:rank], both[rank:]
    write_rows(lambda s: product(basis[s], b[s], TN), out, buffer, sems)


def image_kernel(basis, coeffs, out, buffer, sems):
    write_rows(lambda s: product(basis[s], coeffs[s], TN), out, buffer, sems)


def body(vectors, diagonal, source_basis, transfer, target_basis):
    slots, leaf, rank = source_basis.shape
    vecs = vectors.shape[-1]
    places = Places(SLOT_BITS)
    pair_bits = list(range(places.low_bits))
    nodes, node = (slots, rank, vecs), (rank, vecs)
    basis_shape = (slots, rank, leaf)
    rows_scratch = [pltpu.VMEM((slots, leaf, vecs), jnp.float32), pltpu.SemaphoreType.DMA((slots,))]
    source_t = jnp.swapaxes(source_basis, 1, 2)
    target_t = jnp.swapaxes(target_basis, 1, 2)
    coeffs, source_t, transfer, target_t = call(
        head_kernel,
        [nodes, basis_shape, transfer.shape, basis_shape],
        [
            pltpu.with_memory_space_constraint(x, pltpu.HBM)
            for x in (vectors, source_t, transfer, target_t)
        ],
        [HBM] * 4,
        scratch=[
            pltpu.VMEM(vectors.shape, jnp.float32),
            pltpu.SemaphoreType.DMA((2 * slots + 3,)),
        ],
    )
    meta = places.scalars()
    tops = [SLOT_BITS + places.low_bits + j for j in range(SLOT_BITS)]

    message = (SLOT_BITS * rank + leaf * rank // transfer.shape[3], transfer.shape[3])
    moving = call(
        functools.partial(pick_kernel, tops),
        [message] * slots,
        [meta, transfer, target_t],
        [SMEM, VMEM, VMEM],
    )
    moved = places.across(moving)
    weights = places.reverse_low(diagonal).reshape(slots, leaf)
    top_blocks, basis_t = call(
        arrange_kernel,
        [(SLOT_BITS,) + transfer.shape[1:], basis_shape],
        [meta] + moved,
        [SMEM] + [VMEM] * slots,
    )
    image_basis = places.reverse_low(basis_t)
    square = (slots * rank, slots * rank)
    wide, middle = call(
        fold_kernel,
        [square, square],
        [meta, top_blocks, basis_t, weights],
        [SMEM, VMEM, VMEM, VMEM],
        scratch=[pltpu.VMEM((slots, slots * rank, rank), jnp.float32)],
    )

    for bit in pair_bits:
        partner = places.partner(coeffs, bit)
        last = bit == pair_bits[-1]
        kernel = last_pair_kernel if last else pair_kernel
        blocks = call(
            functools.partial(kernel, SLOT_BITS + bit, bit),
            [node] * slots if last else [nodes],
            [meta, coeffs, partner, transfer],
            [SMEM, VMEM, VMEM, VMEM],
        )
        coeffs = blocks[0]

    blocks = places.across(blocks)
    back = places.across(call(middle_kernel, [node] * slots, [middle] + blocks))
    (coeffs,) = call(top_kernel, [nodes], [wide] + blocks)
    image_coeffs = places.reverse_low(coeffs)
    (forward_image,) = call(
        image_kernel,
        [vectors.shape],
        [image_basis, image_coeffs],
        out_specs=[ANY],
        scratch=rows_scratch,
    )

    for bit in reversed(pair_bits):
        if bit == pair_bits[-1]:
            kernel, operands = first_part_kernel, back
        else:
            kernel, operands = part_kernel, [kept, arrived]
        sent, kept = call(
            functools.partial(kernel, SLOT_BITS + bit, bit),
            [nodes, nodes],
            [meta, transfer] + operands,
            [SMEM] + [VMEM] * (1 + len(operands)),
        )
        arrived = places.partner(sent, bit)
    (adjoint,) = call(
        tail_kernel,
        [vectors.shape],
        [kept, arrived, transfer, source_t],
        out_specs=[ANY],
        scratch=rows_scratch,
    )
    return forward_image, adjoint


def solution(mesh):
    placed = (
        P(BOTH, None),
        P(BOTH),
        P(BOTH, None, None),
        P(None, BOTH, None, None),
        P(BOTH, None, None),
    )

    return jax.shard_map(
        body, mesh=mesh, in_specs=placed, out_specs=(P(BOTH, None), P(BOTH, None)), check_vma=False
    )
```

```python
import functools

import jax
import jax.numpy as jnp
from jax import lax
from jax.experimental import pallas as pl
from jax.experimental.pallas import tpu as pltpu
from jax.sharding import PartitionSpec as P


SLOT_BITS = 2
SLOTS = 2**SLOT_BITS
BOTH = ("row", "col")
NN, TN, NT = ((1,), (0,)), ((0,), (0,)), ((1,), (1,))
VMEM = pl.BlockSpec(memory_space=pltpu.VMEM)
ANY = pl.BlockSpec(memory_space=pl.ANY)
HBM = pl.BlockSpec(memory_space=pltpu.HBM)


def reverse_bits(value, bits):
    out = 0
    for i in range(bits):
        out = out | ((value >> i) & 1) << (bits - 1 - i)
    return out


class Places:
    def __init__(self, slot_bits):
        self.devices = lax.axis_size("row") * lax.axis_size("col")
        self.low_bits = self.devices.bit_length() - 1 - slot_bits

    def permute(self, block, route):
        return lax.ppermute(block, BOTH, [(d, route(d)) for d in range(self.devices)])

    def partner(self, block, bit):
        return self.permute(block, lambda d: d ^ (1 << bit))

    def reverse_low(self, block):
        low = self.low_bits
        return self.permute(
            block, lambda d: (d >> low) << low | reverse_bits(d & (2**low - 1), low)
        )

    def across(self, blocks):
        return [
            b if k == 0 else self.permute(b, lambda d: d ^ (k << self.low_bits))
            for k, b in enumerate(blocks)
        ]


def place():
    return lax.axis_index("row") * lax.axis_size("col") + lax.axis_index("col")


def low_bits():
    return (lax.axis_size("row") * lax.axis_size("col")).bit_length() - 1 - SLOT_BITS


def met(k):
    return reverse_bits((place() >> low_bits()) ^ k, SLOT_BITS)


def is_upper(bit):
    return (place() >> bit) & 1 == 1


def split(x):
    high = x.astype(jnp.bfloat16)
    return high, (x - high.astype(jnp.float32)).astype(jnp.bfloat16)


def product(a, b, dims):
    (ah, al), (bh, bl) = split(a), split(b)

    def dot(x, y):
        return lax.dot_general(x, y, (dims, ((), ())), preferred_element_type=jnp.float32)

    return dot(ah, bh) + (dot(ah, bl) + dot(al, bh))


def call(kernel, outs, operands, specs=None, out_specs=None, scratch=(), flops=1 << 24):
    shapes = [jax.ShapeDtypeStruct(s, jnp.float32) for s in outs]
    return pl.pallas_call(
        kernel,
        out_shape=shapes,
        in_specs=specs or [VMEM] * len(operands),
        out_specs=out_specs or [VMEM] * len(outs),
        scratch_shapes=list(scratch),
        compiler_params=pltpu.CompilerParams(vmem_limit_bytes=8 << 20),
        cost_estimate=pl.CostEstimate(flops=flops, bytes_accessed=1 << 19, transcendentals=0),
    )(*operands)


def pairs(bit):
    return [(s, s | 1 << bit) for s in range(SLOTS) if not s >> bit & 1]


def head_kernel(vectors_in, basis_in, transfer_in, target_in, out, basis, transfer, target, vectors, sems):
    leaf = basis.shape[2]
    copies = []

    def fetch(source, to):
        copies.append(pltpu.make_async_copy(source, to, sems.at[len(copies)]))
        copies[-1].start()
        return copies[-1]

    slots = []
    for s in range(SLOTS):
        rows = pl.ds(s * leaf, leaf)
        slots.append(
            (fetch(basis_in.at[s], basis.at[s]), fetch(vectors_in.at[rows], vectors.at[rows]))
        )
    first = fetch(transfer_in.at[pl.ds(0, SLOT_BITS)], transfer.at[pl.ds(0, SLOT_BITS)])
    rest = pl.ds(SLOT_BITS, transfer.shape[0] - SLOT_BITS)
    later = [fetch(transfer_in.at[rest], transfer.at[rest]), fetch(target_in, target)]
    c = []
    for s in range(SLOTS):
        for copy in slots[s]:
            copy.wait()
        c.append(product(basis[s], vectors[s * leaf : (s + 1) * leaf], NN))
    first.wait()
    for level in range(SLOT_BITS):
        for low, high in pairs(level):
            both = jnp.concatenate([c[low], c[high]], axis=0)
            c[low] = product(transfer[level, low], both, NN)
            c[high] = product(transfer[level, high], both, NN)
    for s in range(SLOTS):
        out[s] = c[s]
    for copy in later:
        copy.wait()


def join(level, bit, s, own, partner, transfer):
    upper = is_upper(bit)
    lower_half = jnp.where(upper, partner[s], own[s])
    upper_half = jnp.where(upper, own[s], partner[s])
    return product(transfer[level, s], jnp.concatenate([lower_half, upper_half], axis=0), NN)


def pair_kernel(level, bit, own, partner, transfer, out):
    for s in range(SLOTS):
        out[s] = join(level, bit, s, own, partner, transfer)


def last_pair_kernel(level, bit, own, partner, transfer, *outs):
    for k in range(SLOTS):
        outs[k][...] = join(level, bit, met(k), own, partner, transfer)


def pick_kernel(tops, transfer, basis, *outs):
    rank, leaf = basis.shape[1:]
    width = transfer.shape[3]
    for k in range(SLOTS):
        s = met(k)
        parts = [transfer[level, s] for level in tops]
        parts += [basis[s, :, j : j + width] for j in range(0, leaf, width)]
        for j, part in enumerate(parts):
            outs[k][j * rank : (j + 1) * rank] = part


def arrange_kernel(*refs):
    moved, tops, basis = refs[:SLOTS], refs[SLOTS], refs[SLOTS + 1]
    rank, width = tops.shape[2:]
    for k in range(SLOTS):
        s = met(k)
        for j in range(SLOT_BITS):
            tops[j, s] = moved[k][j * rank : (j + 1) * rank]
        for j in range(basis.shape[2] // width):
            row = (SLOT_BITS + j) * rank
            basis[s, :, j * width : (j + 1) * width] = moved[k][row : row + rank]


def fold_kernel(tops, basis, weights, wide, middle, columns):
    rank = basis.shape[1]
    blocks = [tops[0, s] for s in range(SLOTS)]
    high = 1 << (SLOT_BITS - 1)
    sources = [[s & ~high, s | high] for s in range(SLOTS)]
    for j in range(1, SLOT_BITS):
        bit = 1 << (SLOT_BITS - 1 - j)
        old, old_sources = blocks, sources
        blocks, sources = [], []
        for s in range(SLOTS):
            halves = [
                product(tops[j, s][:, e * rank : (e + 1) * rank], old[q], NN)
                for e, q in enumerate((s & ~bit, s | bit))
            ]
            blocks.append(jnp.concatenate(halves, axis=1))
            sources.append(old_sources[s & ~bit] + old_sources[s | bit])
    for s in range(SLOTS):
        for at, source in enumerate(sources[s]):
            columns[source, s * rank : (s + 1) * rank] = blocks[s][:, at * rank : (at + 1) * rank]
    ordered = jnp.concatenate([columns[met(k)] for k in range(SLOTS)], axis=1)
    wide[...] = ordered
    inner = []
    for s in range(SLOTS):
        gram = product(basis[s] * weights[s : s + 1, :], basis[s], NT)
        inner.append(product(gram, ordered[s * rank : (s + 1) * rank], NN))
    middle[...] = product(ordered, jnp.concatenate(inner, axis=0), TN)


def middle_kernel(middle, *refs):
    blocks, outs = refs[:SLOTS], refs[SLOTS:]
    rank = blocks[0].shape[0]
    out = product(middle[...], jnp.concatenate([b[...] for b in blocks], axis=0), NN)
    for k in range(SLOTS):
        outs[k][...] = out[k * rank : (k + 1) * rank]


def top_kernel(wide, *refs):
    blocks, out = refs[:SLOTS], refs[SLOTS]
    rank = blocks[0].shape[0]
    rows = product(wide[...], jnp.concatenate([b[...] for b in blocks], axis=0), NN)
    for s in range(SLOTS):
        out[s] = rows[s * rank : (s + 1) * rank]


def part(level, bit, s, block, transfer, sent, kept):
    upper = is_upper(bit)
    out = product(transfer[level, s], block, TN)
    rank = sent.shape[1]
    sent[s] = jnp.where(upper, out[:rank], out[rank:])
    kept[s] = jnp.where(upper, out[rank:], out[:rank])


def first_part_kernel(level, bit, transfer, *refs):
    for k in range(SLOTS):
        part(level, bit, met(k), refs[k][...], transfer, *refs[SLOTS:])


def part_kernel(level, bit, transfer, kept_in, arrived, sent, kept):
    for s in range(SLOTS):
        part(level, bit, s, kept_in[s] + arrived[s], transfer, sent, kept)


def write_rows(rows, out, buffer, sems):
    copies = []
    for s in range(SLOTS):
        leaf = buffer.shape[1]
        buffer[s] = rows(s)
        copies.append(
            pltpu.make_async_copy(buffer.at[s], out.at[pl.ds(s * leaf, leaf)], sems.at[s])
        )
        copies[-1].start()
    for copy in copies:
        copy.wait()


def tail_kernel(kept, arrived, transfer, basis, out, buffer, sems):
    b = [kept[s] + arrived[s] for s in range(SLOTS)]
    rank = b[0].shape[0]
    for level in reversed(range(SLOT_BITS)):
        for low, high in pairs(level):
            blocks = jnp.concatenate([transfer[level, low], transfer[level, high]], axis=0)
            both = product(blocks, jnp.concatenate([b[low], b[high]], axis=0), TN)
            b[low], b[high] = both[:rank], both[rank:]
    write_rows(lambda s: product(basis[s], b[s], TN), out, buffer, sems)


def image_kernel(basis, coeffs, out, buffer, sems):
    write_rows(lambda s: product(basis[s], coeffs[s], TN), out, buffer, sems)


def body(vectors, diagonal, source_basis, transfer, target_basis):
    slots, leaf, rank = source_basis.shape
    vecs = vectors.shape[-1]
    places = Places(SLOT_BITS)
    pair_bits = list(range(places.low_bits))
    nodes, node = (slots, rank, vecs), (rank, vecs)
    basis_shape = (slots, rank, leaf)
    rows_scratch = [pltpu.VMEM((slots, leaf, vecs), jnp.float32), pltpu.SemaphoreType.DMA((slots,))]
    source_t = jnp.swapaxes(source_basis, 1, 2)
    target_t = jnp.swapaxes(target_basis, 1, 2)
    coeffs, source_t, transfer, target_t = call(
        head_kernel,
        [nodes, basis_shape, transfer.shape, basis_shape],
        [
            pltpu.with_memory_space_constraint(x, pltpu.HBM)
            for x in (vectors, source_t, transfer, target_t)
        ],
        [HBM] * 4,
        scratch=[
            pltpu.VMEM(vectors.shape, jnp.float32),
            pltpu.SemaphoreType.DMA((2 * slots + 3,)),
        ],
    )
    tops = [SLOT_BITS + places.low_bits + j for j in range(SLOT_BITS)]

    message = (SLOT_BITS * rank + leaf * rank // transfer.shape[3], transfer.shape[3])
    moving = call(functools.partial(pick_kernel, tops), [message] * slots, [transfer, target_t])
    moved = places.across(moving)
    weights = places.reverse_low(diagonal).reshape(slots, leaf)
    top_blocks, basis_t = call(
        arrange_kernel, [(SLOT_BITS,) + transfer.shape[1:], basis_shape], moved
    )
    image_basis = places.reverse_low(basis_t)
    square = (slots * rank, slots * rank)
    wide, middle = call(
        fold_kernel,
        [square, square],
        [top_blocks, basis_t, weights],
        scratch=[pltpu.VMEM((slots, slots * rank, rank), jnp.float32)],
    )

    for bit in pair_bits:
        partner = places.partner(coeffs, bit)
        last = bit == pair_bits[-1]
        kernel = last_pair_kernel if last else pair_kernel
        blocks = call(
            functools.partial(kernel, SLOT_BITS + bit, bit),
            [node] * slots if last else [nodes],
            [coeffs, partner, transfer],
        )
        coeffs = blocks[0]

    blocks = places.across(blocks)
    back = places.across(call(middle_kernel, [node] * slots, [middle] + blocks))
    (coeffs,) = call(top_kernel, [nodes], [wide] + blocks)
    image_coeffs = places.reverse_low(coeffs)
    (forward_image,) = call(
        image_kernel,
        [vectors.shape],
        [image_basis, image_coeffs],
        out_specs=[ANY],
        scratch=rows_scratch,
    )

    for bit in reversed(pair_bits):
        if bit == pair_bits[-1]:
            kernel, operands = first_part_kernel, back
        else:
            kernel, operands = part_kernel, [kept, arrived]
        sent, kept = call(
            functools.partial(kernel, SLOT_BITS + bit, bit), [nodes, nodes], [transfer] + operands
        )
        arrived = places.partner(sent, bit)
    (adjoint,) = call(
        tail_kernel,
        [vectors.shape],
        [kept, arrived, transfer, source_t],
        out_specs=[ANY],
        scratch=rows_scratch,
    )
    return forward_image, adjoint


def solution(mesh):
    placed = (
        P(BOTH, None),
        P(BOTH),
        P(BOTH, None, None),
        P(None, BOTH, None, None),
        P(BOTH, None, None),
    )

    return jax.shard_map(
        body, mesh=mesh, in_specs=placed, out_specs=(P(BOTH, None), P(BOTH, None)), check_vma=False
    )
```

```python
import functools

import jax
import jax.numpy as jnp
from jax import lax
from jax.experimental import pallas as pl
from jax.experimental.pallas import tpu as pltpu
from jax.sharding import PartitionSpec as P


SLOT_BITS = 2
SLOTS = 2**SLOT_BITS
BOTH = ("row", "col")
NN, TN, NT = ((1,), (0,)), ((0,), (0,)), ((1,), (1,))
VMEM = pl.BlockSpec(memory_space=pltpu.VMEM)
ANY = pl.BlockSpec(memory_space=pl.ANY)
HBM = pl.BlockSpec(memory_space=pltpu.HBM)


def reverse_bits(value, bits):
    out = 0
    for i in range(bits):
        out = out | ((value >> i) & 1) << (bits - 1 - i)
    return out


class Places:
    def __init__(self, slot_bits):
        self.devices = lax.axis_size("row") * lax.axis_size("col")
        self.low_bits = self.devices.bit_length() - 1 - slot_bits

    def permute(self, block, route):
        return lax.ppermute(block, BOTH, [(d, route(d)) for d in range(self.devices)])

    def partner(self, block, bit):
        return self.permute(block, lambda d: d ^ (1 << bit))

    def reverse_low(self, block):
        low = self.low_bits
        return self.permute(
            block, lambda d: (d >> low) << low | reverse_bits(d & (2**low - 1), low)
        )

    def across(self, blocks):
        return [
            b if k == 0 else self.permute(b, lambda d: d ^ (k << self.low_bits))
            for k, b in enumerate(blocks)
        ]


def place():
    return lax.axis_index("row") * lax.axis_size("col") + lax.axis_index("col")


def low_bits():
    return (lax.axis_size("row") * lax.axis_size("col")).bit_length() - 1 - SLOT_BITS


def met(k):
    return reverse_bits((place() >> low_bits()) ^ k, SLOT_BITS)


def is_upper(bit):
    return (place() >> bit) & 1 == 1


def split(x):
    high = x.astype(jnp.bfloat16)
    return high, (x - high.astype(jnp.float32)).astype(jnp.bfloat16)


def product(a, b, dims):
    (ah, al), (bh, bl) = split(a), split(b)

    def dot(x, y):
        return lax.dot_general(x, y, (dims, ((), ())), preferred_element_type=jnp.float32)

    return dot(ah, bh) + (dot(ah, bl) + dot(al, bh))


def call(kernel, outs, operands, specs=None, out_specs=None, scratch=(), flops=1 << 24):
    shapes = [jax.ShapeDtypeStruct(s, jnp.float32) for s in outs]
    return pl.pallas_call(
        kernel,
        out_shape=shapes,
        in_specs=specs or [VMEM] * len(operands),
        out_specs=out_specs or [VMEM] * len(outs),
        scratch_shapes=list(scratch),
        compiler_params=pltpu.CompilerParams(vmem_limit_bytes=8 << 20),
        cost_estimate=pl.CostEstimate(flops=flops, bytes_accessed=1 << 19, transcendentals=0),
    )(*operands)


def pairs(bit):
    return [(s, s | 1 << bit) for s in range(SLOTS) if not s >> bit & 1]


def head_kernel(vectors_in, basis_in, transfer_in, target_in, out, basis, transfer, target, vectors, sems):
    leaf = basis.shape[2]
    copies = []

    def fetch(source, to):
        copies.append(pltpu.make_async_copy(source, to, sems.at[len(copies)]))
        copies[-1].start()
        return copies[-1]

    slots = []
    for s in range(SLOTS):
        rows = pl.ds(s * leaf, leaf)
        slots.append(
            (fetch(basis_in.at[s], basis.at[s]), fetch(vectors_in.at[rows], vectors.at[rows]))
        )
    first = fetch(transfer_in.at[pl.ds(0, SLOT_BITS)], transfer.at[pl.ds(0, SLOT_BITS)])
    rest = pl.ds(SLOT_BITS, transfer.shape[0] - SLOT_BITS)
    later = [fetch(transfer_in.at[rest], transfer.at[rest]), fetch(target_in, target)]
    c = []
    for s in range(SLOTS):
        for copy in slots[s]:
            copy.wait()
        c.append(product(basis[s], vectors[s * leaf : (s + 1) * leaf], NN))
    first.wait()
    for level in range(SLOT_BITS):
        for low, high in pairs(level):
            both = jnp.concatenate([c[low], c[high]], axis=0)
            c[low] = product(transfer[level, low], both, NN)
            c[high] = product(transfer[level, high], both, NN)
    for s in range(SLOTS):
        out[s] = c[s]
    for copy in later:
        copy.wait()


def join(level, bit, s, own, partner, transfer):
    upper = is_upper(bit)
    lower_half = jnp.where(upper, partner[s], own[s])
    upper_half = jnp.where(upper, own[s], partner[s])
    return product(transfer[level, s], jnp.concatenate([lower_half, upper_half], axis=0), NN)


def pair_kernel(level, bit, own, partner, transfer, out):
    for s in range(SLOTS):
        out[s] = join(level, bit, s, own, partner, transfer)


def last_pair_kernel(level, bit, own, partner, transfer, *outs):
    for k in range(SLOTS):
        outs[k][...] = join(level, bit, met(k), own, partner, transfer)


def pick_kernel(tops, transfer, basis, *outs):
    rank, leaf = basis.shape[1:]
    width = transfer.shape[3]
    for k in range(SLOTS):
        s = met(k)
        parts = [transfer[level, s] for level in tops]
        parts += [basis[s, :, j : j + width] for j in range(0, leaf, width)]
        for j, part in enumerate(parts):
            outs[k][j * rank : (j + 1) * rank] = part


def arrange_kernel(*refs):
    moved, tops, basis = refs[:SLOTS], refs[SLOTS], refs[SLOTS + 1]
    rank, width = tops.shape[2:]
    for k in range(SLOTS):
        s = met(k)
        for j in range(SLOT_BITS):
            tops[j, s] = moved[k][j * rank : (j + 1) * rank]
        for j in range(basis.shape[2] // width):
            row = (SLOT_BITS + j) * rank
            basis[s, :, j * width : (j + 1) * width] = moved[k][row : row + rank]


def fold_kernel(tops, basis, weights, wide, middle, columns):
    rank = basis.shape[1]
    blocks = [tops[0, s] for s in range(SLOTS)]
    high = 1 << (SLOT_BITS - 1)
    sources = [[s & ~high, s | high] for s in range(SLOTS)]
    for j in range(1, SLOT_BITS):
        bit = 1 << (SLOT_BITS - 1 - j)
        old, old_sources = blocks, sources
        blocks, sources = [], []
        for s in range(SLOTS):
            halves = [
                product(tops[j, s][:, e * rank : (e + 1) * rank], old[q], NN)
                for e, q in enumerate((s & ~bit, s | bit))
            ]
            blocks.append(jnp.concatenate(halves, axis=1))
            sources.append(old_sources[s & ~bit] + old_sources[s | bit])
    for s in range(SLOTS):
        for at, source in enumerate(sources[s]):
            columns[source, s * rank : (s + 1) * rank] = blocks[s][:, at * rank : (at + 1) * rank]
    ordered = jnp.concatenate([columns[met(k)] for k in range(SLOTS)], axis=1)
    wide[...] = ordered
    inner = []
    for s in range(SLOTS):
        gram = product(basis[s] * weights[s : s + 1, :], basis[s], NT)
        inner.append(product(gram, ordered[s * rank : (s + 1) * rank], NN))
    middle[...] = product(ordered, jnp.concatenate(inner, axis=0), TN)


def middle_kernel(middle, *refs):
    blocks, outs = refs[:SLOTS], refs[SLOTS:]
    rank = blocks[0].shape[0]
    out = product(middle[...], jnp.concatenate([b[...] for b in blocks], axis=0), NN)
    for k in range(SLOTS):
        outs[k][...] = out[k * rank : (k + 1) * rank]


def top_kernel(wide, *refs):
    blocks, out = refs[:SLOTS], refs[SLOTS]
    rank = blocks[0].shape[0]
    rows = product(wide[...], jnp.concatenate([b[...] for b in blocks], axis=0), NN)
    for s in range(SLOTS):
        out[s] = rows[s * rank : (s + 1) * rank]


def part(level, bit, s, block, transfer, sent, kept):
    upper = is_upper(bit)
    out = product(transfer[level, s], block, TN)
    rank = sent.shape[1]
    sent[s] = jnp.where(upper, out[:rank], out[rank:])
    kept[s] = jnp.where(upper, out[rank:], out[:rank])


def first_part_kernel(level, bit, transfer, *refs):
    for k in range(SLOTS):
        part(level, bit, met(k), refs[k][...], transfer, *refs[SLOTS:])


def part_kernel(level, bit, transfer, kept_in, arrived, sent, kept):
    for s in range(SLOTS):
        part(level, bit, s, kept_in[s] + arrived[s], transfer, sent, kept)


def tail_kernel(
    kept, arrived, transfer, basis, image_basis, image_coeffs, image, adjoint, buffers, sems
):
    leaf = buffers.shape[2]
    copies = []

    def write(out, j, s, rows):
        buffers[j, s] = rows
        copies.append(
            pltpu.make_async_copy(buffers.at[j, s], out.at[pl.ds(s * leaf, leaf)], sems.at[j, s])
        )
        copies[-1].start()

    b = [kept[s] + arrived[s] for s in range(SLOTS)]
    rank = b[0].shape[0]
    for level in reversed(range(SLOT_BITS)):
        for low, high in pairs(level):
            blocks = jnp.concatenate([transfer[level, low], transfer[level, high]], axis=0)
            both = product(blocks, jnp.concatenate([b[low], b[high]], axis=0), TN)
            b[low], b[high] = both[:rank], both[rank:]
    for s in range(SLOTS):
        write(adjoint, 0, s, product(basis[s], b[s], TN))
    for s in range(SLOTS):
        write(image, 1, s, product(image_basis[s], image_coeffs[s], TN))
    for copy in copies:
        copy.wait()


def body(vectors, diagonal, source_basis, transfer, target_basis):
    slots, leaf, rank = source_basis.shape
    vecs = vectors.shape[-1]
    places = Places(SLOT_BITS)
    pair_bits = list(range(places.low_bits))
    nodes, node = (slots, rank, vecs), (rank, vecs)
    basis_shape = (slots, rank, leaf)
    source_t = jnp.swapaxes(source_basis, 1, 2)
    target_t = jnp.swapaxes(target_basis, 1, 2)
    coeffs, source_t, transfer, target_t = call(
        head_kernel,
        [nodes, basis_shape, transfer.shape, basis_shape],
        [
            pltpu.with_memory_space_constraint(x, pltpu.HBM)
            for x in (vectors, source_t, transfer, target_t)
        ],
        [HBM] * 4,
        scratch=[
            pltpu.VMEM(vectors.shape, jnp.float32),
            pltpu.SemaphoreType.DMA((2 * slots + 3,)),
        ],
    )
    tops = [SLOT_BITS + places.low_bits + j for j in range(SLOT_BITS)]

    message = (SLOT_BITS * rank + leaf * rank // transfer.shape[3], transfer.shape[3])
    moving = call(functools.partial(pick_kernel, tops), [message] * slots, [transfer, target_t])
    moved = places.across(moving)
    weights = places.reverse_low(diagonal).reshape(slots, leaf)
    top_blocks, basis_t = call(
        arrange_kernel, [(SLOT_BITS,) + transfer.shape[1:], basis_shape], moved
    )
    image_basis = places.reverse_low(basis_t)
    square = (slots * rank, slots * rank)
    wide, middle = call(
        fold_kernel,
        [square, square],
        [top_blocks, basis_t, weights],
        scratch=[pltpu.VMEM((slots, slots * rank, rank), jnp.float32)],
    )

    for bit in pair_bits:
        partner = places.partner(coeffs, bit)
        last = bit == pair_bits[-1]
        kernel = last_pair_kernel if last else pair_kernel
        blocks = call(
            functools.partial(kernel, SLOT_BITS + bit, bit),
            [node] * slots if last else [nodes],
            [coeffs, partner, transfer],
        )
        coeffs = blocks[0]

    blocks = places.across(blocks)
    back = places.across(call(middle_kernel, [node] * slots, [middle] + blocks))
    (coeffs,) = call(top_kernel, [nodes], [wide] + blocks)
    image_coeffs = places.reverse_low(coeffs)
    for bit in reversed(pair_bits):
        if bit == pair_bits[-1]:
            kernel, operands = first_part_kernel, back
        else:
            kernel, operands = part_kernel, [kept, arrived]
        sent, kept = call(
            functools.partial(kernel, SLOT_BITS + bit, bit), [nodes, nodes], [transfer] + operands
        )
        arrived = places.partner(sent, bit)
    forward_image, adjoint = call(
        tail_kernel,
        [vectors.shape] * 2,
        [kept, arrived, transfer, source_t, image_basis, image_coeffs],
        out_specs=[ANY] * 2,
        scratch=[
            pltpu.VMEM((2, slots, leaf, vecs), jnp.float32),
            pltpu.SemaphoreType.DMA((2, slots)),
        ],
    )
    return forward_image, adjoint


def solution(mesh):
    placed = (
        P(BOTH, None),
        P(BOTH),
        P(BOTH, None, None),
        P(None, BOTH, None, None),
        P(BOTH, None, None),
    )

    return jax.shard_map(
        body, mesh=mesh, in_specs=placed, out_specs=(P(BOTH, None), P(BOTH, None)), check_vma=False
    )
```

```python
import functools

import jax
import jax.numpy as jnp
from jax import lax
from jax.experimental import pallas as pl
from jax.experimental.pallas import tpu as pltpu
from jax.sharding import PartitionSpec as P


SLOT_BITS = 2
SLOTS = 2**SLOT_BITS
BOTH = ("row", "col")
NN, TN, NT = ((1,), (0,)), ((0,), (0,)), ((1,), (1,))
VMEM = pl.BlockSpec(memory_space=pltpu.VMEM)
ANY = pl.BlockSpec(memory_space=pl.ANY)
HBM = pl.BlockSpec(memory_space=pltpu.HBM)


def reverse_bits(value, bits):
    out = 0
    for i in range(bits):
        out = out | ((value >> i) & 1) << (bits - 1 - i)
    return out


class Places:
    def __init__(self, slot_bits):
        self.devices = lax.axis_size("row") * lax.axis_size("col")
        self.low_bits = self.devices.bit_length() - 1 - slot_bits

    def permute(self, block, route):
        return lax.ppermute(block, BOTH, [(d, route(d)) for d in range(self.devices)])

    def partner(self, block, bit):
        return self.permute(block, lambda d: d ^ (1 << bit))

    def reverse_low(self, block):
        low = self.low_bits
        return self.permute(
            block, lambda d: (d >> low) << low | reverse_bits(d & (2**low - 1), low)
        )

    def flip_top(self, block, bit):
        return self.permute(block, lambda d: d ^ (1 << (self.low_bits + bit)))

    def across(self, blocks):
        return [
            b if k == 0 else self.permute(b, lambda d: d ^ (k << self.low_bits))
            for k, b in enumerate(blocks)
        ]


def place():
    return lax.axis_index("row") * lax.axis_size("col") + lax.axis_index("col")


def low_bits():
    return (lax.axis_size("row") * lax.axis_size("col")).bit_length() - 1 - SLOT_BITS


def met(k):
    return reverse_bits((place() >> low_bits()) ^ k, SLOT_BITS)


def bit_of_place(bit):
    return (place() >> bit) & 1


def is_upper(bit):
    return bit_of_place(bit) == 1


def top_pair():
    return bit_of_place(low_bits()), bit_of_place(low_bits() + 1)


def split(x):
    high = x.astype(jnp.bfloat16)
    return high, (x - high.astype(jnp.float32)).astype(jnp.bfloat16)


def product(a, b, dims):
    (ah, al), (bh, bl) = split(a), split(b)

    def dot(x, y):
        return lax.dot_general(x, y, (dims, ((), ())), preferred_element_type=jnp.float32)

    return dot(ah, bh) + (dot(ah, bl) + dot(al, bh))


def call(kernel, outs, operands, specs=None, out_specs=None, scratch=(), flops=1 << 24):
    shapes = [jax.ShapeDtypeStruct(s, jnp.float32) for s in outs]
    return pl.pallas_call(
        kernel,
        out_shape=shapes,
        in_specs=specs or [VMEM] * len(operands),
        out_specs=out_specs or [VMEM] * len(outs),
        scratch_shapes=list(scratch),
        compiler_params=pltpu.CompilerParams(vmem_limit_bytes=8 << 20),
        cost_estimate=pl.CostEstimate(flops=flops, bytes_accessed=1 << 19, transcendentals=0),
    )(*operands)


def pairs(bit):
    return [(s, s | 1 << bit) for s in range(SLOTS) if not s >> bit & 1]


def store(out, nodes, weights):
    rank = nodes[0].shape[0]
    for s in range(SLOTS):
        out[s * rank : (s + 1) * rank] = nodes[s]
    out[SLOTS * rank :] = weights


def head_kernel(
    vectors_in,
    basis_in,
    transfer_in,
    target_in,
    diagonal_in,
    out,
    basis,
    transfer,
    target,
    diagonal,
    vectors,
    sems,
):
    leaf = basis.shape[2]
    copies = []

    def fetch(source, to):
        copies.append(pltpu.make_async_copy(source, to, sems.at[len(copies)]))
        copies[-1].start()
        return copies[-1]

    slots = []
    for s in range(SLOTS):
        rows = pl.ds(s * leaf, leaf)
        slots.append(
            (fetch(basis_in.at[s], basis.at[s]), fetch(vectors_in.at[rows], vectors.at[rows]))
        )
    first = fetch(transfer_in.at[pl.ds(0, SLOT_BITS)], transfer.at[pl.ds(0, SLOT_BITS)])
    rest = pl.ds(SLOT_BITS, transfer.shape[0] - SLOT_BITS)
    weights = fetch(diagonal_in, diagonal)
    later = [fetch(target_in, target), fetch(transfer_in.at[rest], transfer.at[rest])]
    c = []
    for s in range(SLOTS):
        for copy in slots[s]:
            copy.wait()
        c.append(product(basis[s], vectors[s * leaf : (s + 1) * leaf], NN))
    first.wait()
    for level in range(SLOT_BITS):
        for low, high in pairs(level):
            both = jnp.concatenate([c[low], c[high]], axis=0)
            c[low] = product(transfer[level, low], both, NN)
            c[high] = product(transfer[level, high], both, NN)
    weights.wait()
    store(out, c, diagonal[...])
    for copy in later:
        copy.wait()


def join(level, bit, s, own, partner, transfer):
    rank = transfer.shape[2]
    rows = pl.ds(pl.multiple_of(s * rank, rank), rank)
    upper = is_upper(bit)
    lower_half = jnp.where(upper, partner[rows], own[rows])
    upper_half = jnp.where(upper, own[rows], partner[rows])
    return product(transfer[level, s], jnp.concatenate([lower_half, upper_half], axis=0), NN)


def pair_kernel(level, bit, own, partner, transfer, out):
    nodes = [join(level, bit, s, own, partner, transfer) for s in range(SLOTS)]
    source = partner if bit == 0 else own
    store(out, nodes, source[SLOTS * transfer.shape[2] :])


def last_pair_kernel(level, bit, own, partner, transfer, diagonal, *outs):
    for k in range(SLOTS):
        outs[k][...] = join(level, bit, met(k), own, partner, transfer)
    same = bit_of_place(0) == bit_of_place(bit)
    outs[SLOTS][...] = jnp.where(same, diagonal[...], partner[SLOTS * transfer.shape[2] :])


def tops_of(transfer, levels, s):
    return jnp.concatenate([transfer[level, s] for level in levels], axis=0)


def first_step(read, out):
    x, _ = top_pair()
    for v in range(2):
        out[v] = read((x ^ 1) << 1 | v)


def second_step(read, first, out):
    x, y = top_pair()
    out[x] = read(x << 1 | (y ^ 1))
    out[x ^ 1] = first[y ^ 1]


def settle(read, first, second, write):
    x, y = top_pair()
    write(x << 1 | y, read(x << 1 | y))
    write((x ^ 1) << 1 | y, first[y])
    for w in range(2):
        write(w << 1 | (y ^ 1), second[w])


def basis_first_kernel(basis, out):
    first_step(lambda s: basis[s], out)


def basis_second_kernel(basis, first, out):
    second_step(lambda s: basis[s], first, out)


def basis_settle_kernel(basis, first, second, out):
    def write(s, block):
        out[s] = block

    settle(lambda s: basis[s], first, second, write)


def tops_first_kernel(levels, transfer, out):
    first_step(lambda s: tops_of(transfer, levels, s), out)


def tops_second_kernel(levels, transfer, first, out):
    second_step(lambda s: tops_of(transfer, levels, s), first, out)


def fold_kernel(levels, transfer, first, second, basis, weights, wide, middle, tops, columns):
    rank = basis.shape[1]

    def write(s, block):
        for j in range(SLOT_BITS):
            tops[j, s] = block[j * rank : (j + 1) * rank]

    settle(lambda s: tops_of(transfer, levels, s), first, second, write)
    blocks = [tops[0, s] for s in range(SLOTS)]
    high = 1 << (SLOT_BITS - 1)
    sources = [[s & ~high, s | high] for s in range(SLOTS)]
    for j in range(1, SLOT_BITS):
        bit = 1 << (SLOT_BITS - 1 - j)
        old, old_sources = blocks, sources
        blocks, sources = [], []
        for s in range(SLOTS):
            halves = [
                product(tops[j, s][:, e * rank : (e + 1) * rank], old[q], NN)
                for e, q in enumerate((s & ~bit, s | bit))
            ]
            blocks.append(jnp.concatenate(halves, axis=1))
            sources.append(old_sources[s & ~bit] + old_sources[s | bit])
    for s in range(SLOTS):
        for at, source in enumerate(sources[s]):
            columns[source, s * rank : (s + 1) * rank] = blocks[s][:, at * rank : (at + 1) * rank]
    ordered = jnp.concatenate([columns[met(k)] for k in range(SLOTS)], axis=1)
    wide[...] = ordered
    inner = []
    for s in range(SLOTS):
        rows = weights.shape[0] // SLOTS
        weight = jnp.concatenate([weights[j : j + 1] for j in range(s * rows, (s + 1) * rows)], axis=1)
        gram = product(basis[s] * weight, basis[s], NT)
        inner.append(product(gram, ordered[s * rank : (s + 1) * rank], NN))
    middle[...] = product(ordered, jnp.concatenate(inner, axis=0), TN)


def middle_kernel(middle, *refs):
    blocks, outs = refs[:SLOTS], refs[SLOTS:]
    rank = blocks[0].shape[0]
    out = product(middle[...], jnp.concatenate([b[...] for b in blocks], axis=0), NN)
    for k in range(SLOTS):
        outs[k][...] = out[k * rank : (k + 1) * rank]


def top_kernel(wide, *refs):
    blocks, out = refs[:SLOTS], refs[SLOTS]
    rank = blocks[0].shape[0]
    rows = product(wide[...], jnp.concatenate([b[...] for b in blocks], axis=0), NN)
    for s in range(SLOTS):
        out[s] = rows[s * rank : (s + 1) * rank]


def part(level, bit, s, block, transfer, sent, kept):
    upper = is_upper(bit)
    out = product(transfer[level, s], block, TN)
    rank = sent.shape[1]
    sent[s] = jnp.where(upper, out[:rank], out[rank:])
    kept[s] = jnp.where(upper, out[rank:], out[:rank])


def first_part_kernel(level, bit, transfer, *refs):
    for k in range(SLOTS):
        part(level, bit, met(k), refs[k][...], transfer, *refs[SLOTS:])


def part_kernel(level, bit, transfer, kept_in, arrived, sent, kept):
    for s in range(SLOTS):
        part(level, bit, s, kept_in[s] + arrived[s], transfer, sent, kept)


def write_rows(rows, out, buffer, sems):
    copies = []
    for s in range(SLOTS):
        leaf = buffer.shape[1]
        buffer[s] = rows(s)
        copies.append(
            pltpu.make_async_copy(buffer.at[s], out.at[pl.ds(s * leaf, leaf)], sems.at[s])
        )
        copies[-1].start()
    for copy in copies:
        copy.wait()


def tail_kernel(kept, arrived, transfer, basis, out, buffer, sems):
    b = [kept[s] + arrived[s] for s in range(SLOTS)]
    rank = b[0].shape[0]
    for level in reversed(range(SLOT_BITS)):
        for low, high in pairs(level):
            blocks = jnp.concatenate([transfer[level, low], transfer[level, high]], axis=0)
            both = product(blocks, jnp.concatenate([b[low], b[high]], axis=0), TN)
            b[low], b[high] = both[:rank], both[rank:]
    write_rows(lambda s: product(basis[s], b[s], TN), out, buffer, sems)


def image_kernel(basis, coeffs, out, buffer, sems):
    write_rows(lambda s: product(basis[s], coeffs[s], TN), out, buffer, sems)


def body(vectors, diagonal, source_basis, transfer, target_basis):
    slots, leaf, rank = source_basis.shape
    vecs = vectors.shape[-1]
    places = Places(SLOT_BITS)
    pair_bits = list(range(places.low_bits))
    nodes, node = (slots, rank, vecs), (rank, vecs)
    basis_shape = (slots, rank, leaf)
    rows_scratch = [pltpu.VMEM((slots, leaf, vecs), jnp.float32), pltpu.SemaphoreType.DMA((slots,))]
    source_t = jnp.swapaxes(source_basis, 1, 2)
    target_t = jnp.swapaxes(target_basis, 1, 2)
    lanes = transfer.shape[3]
    diagonal_rows = diagonal.reshape(-1, lanes)
    packed = (slots * rank + diagonal_rows.shape[0], vecs)
    coeffs, source_t, transfer, target_t, diagonal_rows = call(
        head_kernel,
        [packed, basis_shape, transfer.shape, basis_shape, diagonal_rows.shape],
        [
            pltpu.with_memory_space_constraint(x, pltpu.HBM)
            for x in (vectors, source_t, transfer, target_t, diagonal_rows)
        ],
        [HBM] * 5,
        scratch=[
            pltpu.VMEM(vectors.shape, jnp.float32),
            pltpu.SemaphoreType.DMA((2 * slots + 4,)),
        ],
    )
    tops = [SLOT_BITS + places.low_bits + j for j in range(SLOT_BITS)]

    half = (slots // 2, rank, leaf)
    (sent,) = call(basis_first_kernel, [half], [target_t])
    first = places.flip_top(sent, 0)
    (sent,) = call(basis_second_kernel, [half], [target_t, first])
    second = places.flip_top(sent, 1)
    (basis_t,) = call(basis_settle_kernel, [basis_shape], [target_t, first, second])
    image_basis = places.reverse_low(basis_t)
    half = (slots // 2, SLOT_BITS * rank, lanes)
    (sent,) = call(functools.partial(tops_first_kernel, tops), [half], [transfer])
    first = places.flip_top(sent, 0)
    (sent,) = call(functools.partial(tops_second_kernel, tops), [half], [transfer, first])
    second = places.flip_top(sent, 1)

    for bit in pair_bits:
        partner = places.partner(coeffs, bit)
        last = bit == pair_bits[-1]
        kernel = last_pair_kernel if last else pair_kernel
        blocks = call(
            functools.partial(kernel, SLOT_BITS + bit, bit),
            [node] * slots + [diagonal_rows.shape] if last else [packed],
            [coeffs, partner, transfer] + ([diagonal_rows] if last else []),
        )
        coeffs = blocks[0]
    *blocks, weights = blocks
    if places.low_bits // 2 != 1:
        weights = places.reverse_low(diagonal).reshape(diagonal_rows.shape)

    square = (slots * rank, slots * rank)
    wide, middle = call(
        functools.partial(fold_kernel, tops),
        [square, square],
        [transfer, first, second, basis_t, weights],
        scratch=[
            pltpu.VMEM((SLOT_BITS, slots, rank, lanes), jnp.float32),
            pltpu.VMEM((slots, slots * rank, rank), jnp.float32),
        ],
    )

    blocks = places.across(blocks)
    back = places.across(call(middle_kernel, [node] * slots, [middle] + blocks))
    (coeffs,) = call(top_kernel, [nodes], [wide] + blocks)
    image_coeffs = places.reverse_low(coeffs)
    (forward_image,) = call(
        image_kernel,
        [vectors.shape],
        [image_basis, image_coeffs],
        out_specs=[ANY],
        scratch=rows_scratch,
    )

    for bit in reversed(pair_bits):
        if bit == pair_bits[-1]:
            kernel, operands = first_part_kernel, back
        else:
            kernel, operands = part_kernel, [kept, arrived]
        sent, kept = call(
            functools.partial(kernel, SLOT_BITS + bit, bit), [nodes, nodes], [transfer] + operands
        )
        arrived = places.partner(sent, bit)
    (adjoint,) = call(
        tail_kernel,
        [vectors.shape],
        [kept, arrived, transfer, source_t],
        out_specs=[ANY],
        scratch=rows_scratch,
    )
    return forward_image, adjoint


def solution(mesh):
    placed = (
        P(BOTH, None),
        P(BOTH),
        P(BOTH, None, None),
        P(None, BOTH, None, None),
        P(BOTH, None, None),
    )

    return jax.shard_map(
        body, mesh=mesh, in_specs=placed, out_specs=(P(BOTH, None), P(BOTH, None)), check_vma=False
    )
```

```python
import functools

import jax
import jax.numpy as jnp
from jax import lax
from jax.experimental import pallas as pl
from jax.experimental.pallas import tpu as pltpu
from jax.sharding import PartitionSpec as P


SLOT_BITS = 2
SLOTS = 2**SLOT_BITS
BOTH = ("row", "col")
CROSSING = sorted(range(1, SLOTS), key=lambda k: -k.bit_count())
FORWARD_PIECES = [CROSSING[: SLOTS // 2], CROSSING[SLOTS // 2 :] + [0]]
BACK_PIECES = [[0], CROSSING]
NN, TN, NT = ((1,), (0,)), ((0,), (0,)), ((1,), (1,))
VMEM = pl.BlockSpec(memory_space=pltpu.VMEM)
ANY = pl.BlockSpec(memory_space=pl.ANY)
HBM = pl.BlockSpec(memory_space=pltpu.HBM)


def reverse_bits(value, bits):
    out = 0
    for i in range(bits):
        out = out | ((value >> i) & 1) << (bits - 1 - i)
    return out


class Places:
    def __init__(self, slot_bits):
        self.devices = lax.axis_size("row") * lax.axis_size("col")
        self.low_bits = self.devices.bit_length() - 1 - slot_bits

    def permute(self, block, route):
        return lax.ppermute(block, BOTH, [(d, route(d)) for d in range(self.devices)])

    def partner(self, block, bit):
        return self.permute(block, lambda d: d ^ (1 << bit))

    def reverse_low(self, block):
        low = self.low_bits
        return self.permute(
            block, lambda d: (d >> low) << low | reverse_bits(d & (2**low - 1), low)
        )

    def flip_top(self, block, bit):
        return self.permute(block, lambda d: d ^ (1 << (self.low_bits + bit)))

    def across(self, blocks):
        return [
            b if k == 0 else self.permute(b, lambda d: d ^ (k << self.low_bits))
            for k, b in enumerate(blocks)
        ]


def place():
    return lax.axis_index("row") * lax.axis_size("col") + lax.axis_index("col")


def low_bits():
    return (lax.axis_size("row") * lax.axis_size("col")).bit_length() - 1 - SLOT_BITS


def met(k):
    return reverse_bits((place() >> low_bits()) ^ k, SLOT_BITS)


def bit_of_place(bit):
    return (place() >> bit) & 1


def is_upper(bit):
    return bit_of_place(bit) == 1


def top_pair():
    return bit_of_place(low_bits()), bit_of_place(low_bits() + 1)


def split(x):
    high = x.astype(jnp.bfloat16)
    return high, (x - high.astype(jnp.float32)).astype(jnp.bfloat16)


def product(a, b, dims):
    (ah, al), (bh, bl) = split(a), split(b)

    def dot(x, y):
        return lax.dot_general(x, y, (dims, ((), ())), preferred_element_type=jnp.float32)

    return dot(ah, bh) + (dot(ah, bl) + dot(al, bh))


def call(kernel, outs, operands, specs=None, out_specs=None, scratch=(), flops=1 << 24):
    shapes = [jax.ShapeDtypeStruct(s, jnp.float32) for s in outs]
    return pl.pallas_call(
        kernel,
        out_shape=shapes,
        in_specs=specs or [VMEM] * len(operands),
        out_specs=out_specs or [VMEM] * len(outs),
        scratch_shapes=list(scratch),
        compiler_params=pltpu.CompilerParams(vmem_limit_bytes=8 << 20),
        cost_estimate=pl.CostEstimate(flops=flops, bytes_accessed=1 << 19, transcendentals=0),
    )(*operands)


def pairs(bit):
    return [(s, s | 1 << bit) for s in range(SLOTS) if not s >> bit & 1]


def store(out, nodes, weights):
    rank = nodes[0].shape[0]
    for at, node in enumerate(nodes):
        out[at * rank : (at + 1) * rank] = node
    if weights is not None:
        out[len(nodes) * rank :] = weights


def head_kernel(
    vectors_in,
    basis_in,
    transfer_in,
    target_in,
    diagonal_in,
    out,
    basis,
    transfer,
    target,
    diagonal,
    vectors,
    sems,
):
    leaf = basis.shape[2]
    copies = []

    def fetch(source, to):
        copies.append(pltpu.make_async_copy(source, to, sems.at[len(copies)]))
        copies[-1].start()
        return copies[-1]

    slots = []
    for s in range(SLOTS):
        rows = pl.ds(s * leaf, leaf)
        slots.append(
            (fetch(basis_in.at[s], basis.at[s]), fetch(vectors_in.at[rows], vectors.at[rows]))
        )
    first = fetch(transfer_in.at[pl.ds(0, SLOT_BITS)], transfer.at[pl.ds(0, SLOT_BITS)])
    rest = pl.ds(SLOT_BITS, transfer.shape[0] - SLOT_BITS)
    weights = fetch(diagonal_in, diagonal)
    later = [fetch(target_in, target), fetch(transfer_in.at[rest], transfer.at[rest])]
    c = []
    for s in range(SLOTS):
        for copy in slots[s]:
            copy.wait()
        c.append(product(basis[s], vectors[s * leaf : (s + 1) * leaf], NN))
    first.wait()
    for level in range(SLOT_BITS):
        for low, high in pairs(level):
            both = jnp.concatenate([c[low], c[high]], axis=0)
            c[low] = product(transfer[level, low], both, NN)
            c[high] = product(transfer[level, high], both, NN)
    weights.wait()
    store(out, c, diagonal[...])
    for copy in later:
        copy.wait()


def join(level, bit, s, at, own, partner, transfer):
    rank = transfer.shape[2]
    rows = pl.ds(pl.multiple_of(at * rank, rank), rank)
    upper = is_upper(bit)
    lower_half = jnp.where(upper, partner[rows], own[rows])
    upper_half = jnp.where(upper, own[rows], partner[rows])
    return product(transfer[level, s], jnp.concatenate([lower_half, upper_half], axis=0), NN)


def weights_of(bit, own, partner, rank):
    return (partner if bit == 0 else own)[SLOTS * rank :]


def pair_kernel(level, bit, own, partner, transfer, out):
    nodes = [join(level, bit, s, s, own, partner, transfer) for s in range(SLOTS)]
    store(out, nodes, weights_of(bit, own, partner, transfer.shape[2]))


def cutting_pair_kernel(level, bit, own, partner, transfer, *outs):
    for j, piece in enumerate(FORWARD_PIECES):
        nodes = [join(level, bit, met(k), met(k), own, partner, transfer) for k in piece]
        weights = weights_of(bit, own, partner, transfer.shape[2]) if j == 0 else None
        store(outs[j], nodes, weights)


def last_pair_kernel(level, bit, piece, own, partner, transfer, *outs):
    for at, k in enumerate(piece):
        outs[at][...] = join(level, bit, met(k), at, own, partner, transfer)


def weights_kernel(bit, rows, diagonal, partner, out):
    same = bit_of_place(0) == bit_of_place(bit)
    out[...] = jnp.where(same, diagonal[...], partner[rows:])


def tops_of(transfer, levels, s):
    return jnp.concatenate([transfer[level, s] for level in levels], axis=0)


def first_step(read, out):
    x, _ = top_pair()
    for v in range(2):
        out[v] = read((x ^ 1) << 1 | v)


def second_step(read, first, out):
    x, y = top_pair()
    out[x] = read(x << 1 | (y ^ 1))
    out[x ^ 1] = first[y ^ 1]


def settle(read, first, second, write):
    x, y = top_pair()
    write(x << 1 | y, read(x << 1 | y))
    write((x ^ 1) << 1 | y, first[y])
    for w in range(2):
        write(w << 1 | (y ^ 1), second[w])


def basis_first_kernel(basis, out):
    first_step(lambda s: basis[s], out)


def basis_second_kernel(basis, first, out):
    second_step(lambda s: basis[s], first, out)


def basis_settle_kernel(basis, first, second, out):
    def write(s, block):
        out[s] = block

    settle(lambda s: basis[s], first, second, write)


def tops_first_kernel(levels, transfer, out):
    first_step(lambda s: tops_of(transfer, levels, s), out)


def tops_second_kernel(levels, transfer, first, out):
    second_step(lambda s: tops_of(transfer, levels, s), first, out)


def fold_kernel(levels, transfer, first, second, basis, weights, wide, middle, tops, columns):
    rank = basis.shape[1]

    def write(s, block):
        for j in range(SLOT_BITS):
            tops[j, s] = block[j * rank : (j + 1) * rank]

    settle(lambda s: tops_of(transfer, levels, s), first, second, write)
    blocks = [tops[0, s] for s in range(SLOTS)]
    high = 1 << (SLOT_BITS - 1)
    sources = [[s & ~high, s | high] for s in range(SLOTS)]
    for j in range(1, SLOT_BITS):
        bit = 1 << (SLOT_BITS - 1 - j)
        old, old_sources = blocks, sources
        blocks, sources = [], []
        for s in range(SLOTS):
            halves = [
                product(tops[j, s][:, e * rank : (e + 1) * rank], old[q], NN)
                for e, q in enumerate((s & ~bit, s | bit))
            ]
            blocks.append(jnp.concatenate(halves, axis=1))
            sources.append(old_sources[s & ~bit] + old_sources[s | bit])
    for s in range(SLOTS):
        for at, source in enumerate(sources[s]):
            columns[source, s * rank : (s + 1) * rank] = blocks[s][:, at * rank : (at + 1) * rank]
    ordered = jnp.concatenate([columns[met(k)] for k in range(SLOTS)], axis=1)
    wide[...] = ordered
    inner = []
    for s in range(SLOTS):
        rows = weights.shape[0] // SLOTS
        weight = jnp.concatenate([weights[j : j + 1] for j in range(s * rows, (s + 1) * rows)], axis=1)
        gram = product(basis[s] * weight, basis[s], NT)
        inner.append(product(gram, ordered[s * rank : (s + 1) * rank], NN))
    middle[...] = product(ordered, jnp.concatenate(inner, axis=0), TN)


def middle_kernel(middle, *refs):
    blocks, outs = refs[:SLOTS], refs[SLOTS:]
    rank = blocks[0].shape[0]
    out = product(middle[...], jnp.concatenate([b[...] for b in blocks], axis=0), NN)
    for k in range(SLOTS):
        outs[k][...] = out[k * rank : (k + 1) * rank]


def top_kernel(wide, *refs):
    blocks, out = refs[:SLOTS], refs[SLOTS]
    rank = blocks[0].shape[0]
    rows = product(wide[...], jnp.concatenate([b[...] for b in blocks], axis=0), NN)
    for s in range(SLOTS):
        out[s] = rows[s * rank : (s + 1) * rank]


def part(level, bit, s, at, block, transfer, sent, kept):
    upper = is_upper(bit)
    out = product(transfer[level, s], block, TN)
    rank = sent.shape[1]
    sent[at] = jnp.where(upper, out[:rank], out[rank:])
    kept[at] = jnp.where(upper, out[rank:], out[:rank])


def first_part_kernel(level, bit, piece, transfer, *refs):
    sent, kept = refs[len(piece) :]
    for at, k in enumerate(piece):
        part(level, bit, met(k), at, refs[at][...], transfer, sent, kept)


def joining_part_kernel(level, bit, transfer, *refs):
    sent, kept = refs[-2:]
    for j, piece in enumerate(BACK_PIECES):
        kept_in, arrived = refs[2 * j : 2 * j + 2]
        for at, k in enumerate(piece):
            s = met(k)
            part(level, bit, s, s, kept_in[at] + arrived[at], transfer, sent, kept)


def part_kernel(level, bit, transfer, kept_in, arrived, sent, kept):
    for s in range(SLOTS):
        part(level, bit, s, s, kept_in[s] + arrived[s], transfer, sent, kept)


def write_rows(rows, out, buffer, sems):
    copies = []
    for s in range(SLOTS):
        leaf = buffer.shape[1]
        buffer[s] = rows(s)
        copies.append(
            pltpu.make_async_copy(buffer.at[s], out.at[pl.ds(s * leaf, leaf)], sems.at[s])
        )
        copies[-1].start()
    for copy in copies:
        copy.wait()


def tail_kernel(kept, arrived, transfer, basis, out, buffer, sems):
    b = [kept[s] + arrived[s] for s in range(SLOTS)]
    rank = b[0].shape[0]
    for level in reversed(range(SLOT_BITS)):
        for low, high in pairs(level):
            blocks = jnp.concatenate([transfer[level, low], transfer[level, high]], axis=0)
            both = product(blocks, jnp.concatenate([b[low], b[high]], axis=0), TN)
            b[low], b[high] = both[:rank], both[rank:]
    write_rows(lambda s: product(basis[s], b[s], TN), out, buffer, sems)


def image_kernel(basis, coeffs, out, buffer, sems):
    write_rows(lambda s: product(basis[s], coeffs[s], TN), out, buffer, sems)


def body(vectors, diagonal, source_basis, transfer, target_basis):
    slots, leaf, rank = source_basis.shape
    vecs = vectors.shape[-1]
    places = Places(SLOT_BITS)
    pair_bits = list(range(places.low_bits))
    nodes, node = (slots, rank, vecs), (rank, vecs)
    basis_shape = (slots, rank, leaf)
    rows_scratch = [pltpu.VMEM((slots, leaf, vecs), jnp.float32), pltpu.SemaphoreType.DMA((slots,))]
    source_t = jnp.swapaxes(source_basis, 1, 2)
    target_t = jnp.swapaxes(target_basis, 1, 2)
    lanes = transfer.shape[3]
    diagonal_rows = diagonal.reshape(-1, lanes)
    packed = (slots * rank + diagonal_rows.shape[0], vecs)
    coeffs, source_t, transfer, target_t, diagonal_rows = call(
        head_kernel,
        [packed, basis_shape, transfer.shape, basis_shape, diagonal_rows.shape],
        [
            pltpu.with_memory_space_constraint(x, pltpu.HBM)
            for x in (vectors, source_t, transfer, target_t, diagonal_rows)
        ],
        [HBM] * 5,
        scratch=[
            pltpu.VMEM(vectors.shape, jnp.float32),
            pltpu.SemaphoreType.DMA((2 * slots + 4,)),
        ],
    )
    tops = [SLOT_BITS + places.low_bits + j for j in range(SLOT_BITS)]

    half = (slots // 2, rank, leaf)
    (sent,) = call(basis_first_kernel, [half], [target_t])
    first = places.flip_top(sent, 0)
    (sent,) = call(basis_second_kernel, [half], [target_t, first])
    second = places.flip_top(sent, 1)
    (basis_t,) = call(basis_settle_kernel, [basis_shape], [target_t, first, second])
    image_basis = places.reverse_low(basis_t)
    half = (slots // 2, SLOT_BITS * rank, lanes)
    (sent,) = call(functools.partial(tops_first_kernel, tops), [half], [transfer])
    first = places.flip_top(sent, 0)
    (sent,) = call(functools.partial(tops_second_kernel, tops), [half], [transfer, first])
    second = places.flip_top(sent, 1)

    *early_bits, last_bit = pair_bits
    weight_rows = diagonal_rows.shape[0]
    for bit in early_bits:
        partner = places.partner(coeffs, bit)
        cut = bit == early_bits[-1]
        rows = [len(piece) * rank for piece in FORWARD_PIECES]
        rows[0] += weight_rows
        coeffs, *others = call(
            functools.partial(cutting_pair_kernel if cut else pair_kernel, SLOT_BITS + bit, bit),
            [(n, vecs) for n in rows] if cut else [packed],
            [coeffs, partner, transfer],
        )
    messages = [coeffs] + others
    partners = [places.partner(message, last_bit) for message in messages]
    blocks = {}
    for j, piece in enumerate(FORWARD_PIECES):
        outs = call(
            functools.partial(last_pair_kernel, SLOT_BITS + last_bit, last_bit, piece),
            [node] * len(piece),
            [messages[j], partners[j], transfer],
        )
        blocks.update(zip(piece, outs))
    blocks = [blocks[k] for k in range(SLOTS)]
    if places.low_bits // 2 == 1:
        (weights,) = call(
            functools.partial(weights_kernel, last_bit, len(FORWARD_PIECES[0]) * rank),
            [diagonal_rows.shape],
            [diagonal_rows, partners[0]],
        )
    else:
        weights = places.reverse_low(diagonal).reshape(diagonal_rows.shape)

    square = (slots * rank, slots * rank)
    wide, middle = call(
        functools.partial(fold_kernel, tops),
        [square, square],
        [transfer, first, second, basis_t, weights],
        scratch=[
            pltpu.VMEM((SLOT_BITS, slots, rank, lanes), jnp.float32),
            pltpu.VMEM((slots, slots * rank, rank), jnp.float32),
        ],
    )

    blocks = places.across(blocks)
    back = places.across(call(middle_kernel, [node] * slots, [middle] + blocks))
    (coeffs,) = call(top_kernel, [nodes], [wide] + blocks)
    image_coeffs = places.reverse_low(coeffs)
    (forward_image,) = call(
        image_kernel,
        [vectors.shape],
        [image_basis, image_coeffs],
        out_specs=[ANY],
        scratch=rows_scratch,
    )

    pieces = []
    for piece in BACK_PIECES:
        shape = (len(piece), rank, vecs)
        sent, kept = call(
            functools.partial(first_part_kernel, SLOT_BITS + last_bit, last_bit, piece),
            [shape, shape],
            [transfer] + [back[k] for k in piece],
        )
        pieces += [kept, places.partner(sent, last_bit)]
    for bit in reversed(early_bits):
        sent, kept = call(
            functools.partial(
                joining_part_kernel if bit == early_bits[-1] else part_kernel, SLOT_BITS + bit, bit
            ),
            [nodes, nodes],
            [transfer] + pieces,
        )
        pieces = [kept, places.partner(sent, bit)]
    kept, arrived = pieces
    (adjoint,) = call(
        tail_kernel,
        [vectors.shape],
        [kept, arrived, transfer, source_t],
        out_specs=[ANY],
        scratch=rows_scratch,
    )
    return forward_image, adjoint


def solution(mesh):
    placed = (
        P(BOTH, None),
        P(BOTH),
        P(BOTH, None, None),
        P(None, BOTH, None, None),
        P(BOTH, None, None),
    )

    return jax.shard_map(
        body, mesh=mesh, in_specs=placed, out_specs=(P(BOTH, None), P(BOTH, None)), check_vma=False
    )
```

```python
import functools

import jax
import jax.numpy as jnp
from jax import lax
from jax.experimental import pallas as pl
from jax.experimental.pallas import tpu as pltpu
from jax.sharding import PartitionSpec as P


SLOT_BITS = 2
SLOTS = 2**SLOT_BITS
BOTH = ("row", "col")
CROSSING = sorted(range(1, SLOTS), key=lambda k: -k.bit_count())
FORWARD_PIECES = [CROSSING[: SLOTS // 2], CROSSING[SLOTS // 2 :] + [0]]
BACK_PIECES = [[0], CROSSING]
NN, TN, NT = ((1,), (0,)), ((0,), (0,)), ((1,), (1,))
VMEM = pl.BlockSpec(memory_space=pltpu.VMEM)
ANY = pl.BlockSpec(memory_space=pl.ANY)
HBM = pl.BlockSpec(memory_space=pltpu.HBM)


def reverse_bits(value, bits):
    out = 0
    for i in range(bits):
        out = out | ((value >> i) & 1) << (bits - 1 - i)
    return out


class Places:
    def __init__(self, slot_bits):
        self.devices = lax.axis_size("row") * lax.axis_size("col")
        self.low_bits = self.devices.bit_length() - 1 - slot_bits

    def permute(self, block, route):
        return lax.ppermute(block, BOTH, [(d, route(d)) for d in range(self.devices)])

    def partner(self, block, bit):
        return self.permute(block, lambda d: d ^ (1 << bit))

    def reverse_low(self, block):
        low = self.low_bits
        return self.permute(
            block, lambda d: (d >> low) << low | reverse_bits(d & (2**low - 1), low)
        )

    def flip_top(self, block, bit):
        return self.permute(block, lambda d: d ^ (1 << (self.low_bits + bit)))

    def across(self, blocks):
        return [
            b if k == 0 else self.permute(b, lambda d: d ^ (k << self.low_bits))
            for k, b in enumerate(blocks)
        ]


def place():
    return lax.axis_index("row") * lax.axis_size("col") + lax.axis_index("col")


def low_bits():
    return (lax.axis_size("row") * lax.axis_size("col")).bit_length() - 1 - SLOT_BITS


def met(k):
    return reverse_bits((place() >> low_bits()) ^ k, SLOT_BITS)


def bit_of_place(bit):
    return (place() >> bit) & 1


def is_upper(bit):
    return bit_of_place(bit) == 1


def top_pair():
    return bit_of_place(low_bits()), bit_of_place(low_bits() + 1)


def split(x):
    high = x.astype(jnp.bfloat16)
    return high, (x - high.astype(jnp.float32)).astype(jnp.bfloat16)


def product(a, b, dims):
    (ah, al), (bh, bl) = split(a), split(b)

    def dot(x, y):
        return lax.dot_general(x, y, (dims, ((), ())), preferred_element_type=jnp.float32)

    return dot(ah, bh) + (dot(ah, bl) + dot(al, bh))


def call(kernel, outs, operands, specs=None, out_specs=None, scratch=(), flops=1 << 24):
    shapes = [jax.ShapeDtypeStruct(s, jnp.float32) for s in outs]
    return pl.pallas_call(
        kernel,
        out_shape=shapes,
        in_specs=specs or [VMEM] * len(operands),
        out_specs=out_specs or [VMEM] * len(outs),
        scratch_shapes=list(scratch),
        compiler_params=pltpu.CompilerParams(vmem_limit_bytes=8 << 20),
        cost_estimate=pl.CostEstimate(flops=flops, bytes_accessed=1 << 19, transcendentals=0),
    )(*operands)


def pairs(bit):
    return [(s, s | 1 << bit) for s in range(SLOTS) if not s >> bit & 1]


def store(out, nodes, weights):
    rank = nodes[0].shape[0]
    for at, node in enumerate(nodes):
        out[at * rank : (at + 1) * rank] = node
    if weights is not None:
        out[len(nodes) * rank :] = weights


def head_kernel(
    vectors_in,
    basis_in,
    transfer_in,
    target_in,
    diagonal_in,
    out,
    basis,
    target,
    diagonal,
    transfer,
    vectors,
    sems,
):
    leaf = basis.shape[2]
    copies = []

    def fetch(source, to):
        copies.append(pltpu.make_async_copy(source, to, sems.at[len(copies)]))
        copies[-1].start()
        return copies[-1]

    slots = []
    for s in range(SLOTS):
        rows = pl.ds(s * leaf, leaf)
        slots.append(
            (fetch(basis_in.at[s], basis.at[s]), fetch(vectors_in.at[rows], vectors.at[rows]))
        )
    first = fetch(transfer_in.at[pl.ds(0, SLOT_BITS)], transfer)
    weights = fetch(diagonal_in, diagonal)
    later = fetch(target_in, target)
    c = []
    for s in range(SLOTS):
        for copy in slots[s]:
            copy.wait()
        c.append(product(basis[s], vectors[s * leaf : (s + 1) * leaf], NN))
    first.wait()
    for level in range(SLOT_BITS):
        for low, high in pairs(level):
            both = jnp.concatenate([c[low], c[high]], axis=0)
            c[low] = product(transfer[level, low], both, NN)
            c[high] = product(transfer[level, high], both, NN)
    weights.wait()
    store(out, c, diagonal[...])
    later.wait()


def join(level, bit, s, at, own, partner, transfer):
    rank = transfer.shape[2]
    rows = pl.ds(pl.multiple_of(at * rank, rank), rank)
    upper = is_upper(bit)
    lower_half = jnp.where(upper, partner[rows], own[rows])
    upper_half = jnp.where(upper, own[rows], partner[rows])
    return product(transfer[level, s], jnp.concatenate([lower_half, upper_half], axis=0), NN)


def weights_of(bit, own, partner, rank):
    return (partner if bit == 0 else own)[SLOTS * rank :]


def pair_kernel(level, bit, own, partner, transfer, out):
    nodes = [join(level, bit, s, s, own, partner, transfer) for s in range(SLOTS)]
    store(out, nodes, weights_of(bit, own, partner, transfer.shape[2]))


def cutting_pair_kernel(level, bit, own, partner, transfer, *outs):
    for j, piece in enumerate(FORWARD_PIECES):
        nodes = [join(level, bit, met(k), met(k), own, partner, transfer) for k in piece]
        weights = weights_of(bit, own, partner, transfer.shape[2]) if j == 0 else None
        store(outs[j], nodes, weights)


def last_pair_kernel(level, bit, piece, own, partner, transfer, *outs):
    for at, k in enumerate(piece):
        outs[at][...] = join(level, bit, met(k), at, own, partner, transfer)


def weights_kernel(bit, rows, diagonal, partner, out):
    same = bit_of_place(0) == bit_of_place(bit)
    out[...] = jnp.where(same, diagonal[...], partner[rows:])


def tops_of(transfer, levels, s):
    return jnp.concatenate([transfer[level, s] for level in levels], axis=0)


def first_step(read, out):
    x, _ = top_pair()
    for v in range(2):
        out[v] = read((x ^ 1) << 1 | v)


def second_step(read, first, out):
    x, y = top_pair()
    out[x] = read(x << 1 | (y ^ 1))
    out[x ^ 1] = first[y ^ 1]


def settle(read, first, second, write):
    x, y = top_pair()
    write(x << 1 | y, read(x << 1 | y))
    write((x ^ 1) << 1 | y, first[y])
    for w in range(2):
        write(w << 1 | (y ^ 1), second[w])


def basis_first_kernel(basis, out):
    first_step(lambda s: basis[s], out)


def basis_second_kernel(basis, first, out):
    second_step(lambda s: basis[s], first, out)


def basis_settle_kernel(basis, first, second, out):
    def write(s, block):
        out[s] = block

    settle(lambda s: basis[s], first, second, write)


def tops_first_kernel(levels, transfer, out):
    first_step(lambda s: tops_of(transfer, levels, s), out)


def tops_second_kernel(levels, transfer, first, out):
    second_step(lambda s: tops_of(transfer, levels, s), first, out)


def fold_kernel(levels, transfer, first, second, basis, weights, wide, middle, tops, columns):
    rank = basis.shape[1]

    def write(s, block):
        for j in range(SLOT_BITS):
            tops[j, s] = block[j * rank : (j + 1) * rank]

    settle(lambda s: tops_of(transfer, levels, s), first, second, write)
    blocks = [tops[0, s] for s in range(SLOTS)]
    high = 1 << (SLOT_BITS - 1)
    sources = [[s & ~high, s | high] for s in range(SLOTS)]
    for j in range(1, SLOT_BITS):
        bit = 1 << (SLOT_BITS - 1 - j)
        old, old_sources = blocks, sources
        blocks, sources = [], []
        for s in range(SLOTS):
            halves = [
                product(tops[j, s][:, e * rank : (e + 1) * rank], old[q], NN)
                for e, q in enumerate((s & ~bit, s | bit))
            ]
            blocks.append(jnp.concatenate(halves, axis=1))
            sources.append(old_sources[s & ~bit] + old_sources[s | bit])
    for s in range(SLOTS):
        for at, source in enumerate(sources[s]):
            columns[source, s * rank : (s + 1) * rank] = blocks[s][:, at * rank : (at + 1) * rank]
    ordered = jnp.concatenate([columns[met(k)] for k in range(SLOTS)], axis=1)
    wide[...] = ordered
    inner = []
    for s in range(SLOTS):
        rows = weights.shape[0] // SLOTS
        weight = jnp.concatenate([weights[j : j + 1] for j in range(s * rows, (s + 1) * rows)], axis=1)
        gram = product(basis[s] * weight, basis[s], NT)
        inner.append(product(gram, ordered[s * rank : (s + 1) * rank], NN))
    middle[...] = product(ordered, jnp.concatenate(inner, axis=0), TN)


def middle_kernel(middle, *refs):
    blocks, outs = refs[:SLOTS], refs[SLOTS:]
    rank = blocks[0].shape[0]
    out = product(middle[...], jnp.concatenate([b[...] for b in blocks], axis=0), NN)
    for k in range(SLOTS):
        outs[k][...] = out[k * rank : (k + 1) * rank]


def top_kernel(wide, *refs):
    blocks, out = refs[:SLOTS], refs[SLOTS]
    rank = blocks[0].shape[0]
    rows = product(wide[...], jnp.concatenate([b[...] for b in blocks], axis=0), NN)
    for s in range(SLOTS):
        out[s] = rows[s * rank : (s + 1) * rank]


def part(level, bit, s, at, block, transfer, sent, kept):
    upper = is_upper(bit)
    out = product(transfer[level, s], block, TN)
    rank = sent.shape[1]
    sent[at] = jnp.where(upper, out[:rank], out[rank:])
    kept[at] = jnp.where(upper, out[rank:], out[:rank])


def first_part_kernel(level, bit, piece, transfer, *refs):
    sent, kept = refs[len(piece) :]
    for at, k in enumerate(piece):
        part(level, bit, met(k), at, refs[at][...], transfer, sent, kept)


def joining_part_kernel(level, bit, transfer, *refs):
    sent, kept = refs[-2:]
    for j, piece in enumerate(BACK_PIECES):
        kept_in, arrived = refs[2 * j : 2 * j + 2]
        for at, k in enumerate(piece):
            s = met(k)
            part(level, bit, s, s, kept_in[at] + arrived[at], transfer, sent, kept)


def part_kernel(level, bit, transfer, kept_in, arrived, sent, kept):
    for s in range(SLOTS):
        part(level, bit, s, s, kept_in[s] + arrived[s], transfer, sent, kept)


def write_rows(rows, out, buffer, sems):
    copies = []
    for s in range(SLOTS):
        leaf = buffer.shape[1]
        buffer[s] = rows(s)
        copies.append(
            pltpu.make_async_copy(buffer.at[s], out.at[pl.ds(s * leaf, leaf)], sems.at[s])
        )
        copies[-1].start()
    for copy in copies:
        copy.wait()


def tail_kernel(kept, arrived, transfer, basis, out, buffer, sems):
    b = [kept[s] + arrived[s] for s in range(SLOTS)]
    rank = b[0].shape[0]
    for level in reversed(range(SLOT_BITS)):
        for low, high in pairs(level):
            blocks = jnp.concatenate([transfer[level, low], transfer[level, high]], axis=0)
            both = product(blocks, jnp.concatenate([b[low], b[high]], axis=0), TN)
            b[low], b[high] = both[:rank], both[rank:]
    write_rows(lambda s: product(basis[s], b[s], TN), out, buffer, sems)


def image_kernel(basis, coeffs, out, buffer, sems):
    write_rows(lambda s: product(basis[s], coeffs[s], TN), out, buffer, sems)


def body(vectors, diagonal, source_basis, transfer, target_basis):
    slots, leaf, rank = source_basis.shape
    vecs = vectors.shape[-1]
    places = Places(SLOT_BITS)
    pair_bits = list(range(places.low_bits))
    nodes, node = (slots, rank, vecs), (rank, vecs)
    basis_shape = (slots, rank, leaf)
    rows_scratch = [pltpu.VMEM((slots, leaf, vecs), jnp.float32), pltpu.SemaphoreType.DMA((slots,))]
    source_t = jnp.swapaxes(source_basis, 1, 2)
    target_t = jnp.swapaxes(target_basis, 1, 2)
    lanes = transfer.shape[3]
    diagonal_rows = diagonal.reshape(-1, lanes)
    packed = (slots * rank + diagonal_rows.shape[0], vecs)
    coeffs, source_t, target_t, diagonal_rows = call(
        head_kernel,
        [packed, basis_shape, basis_shape, diagonal_rows.shape],
        [
            pltpu.with_memory_space_constraint(x, pltpu.HBM)
            for x in (vectors, source_t, transfer, target_t, diagonal_rows)
        ],
        [HBM] * 5,
        scratch=[
            pltpu.VMEM((SLOT_BITS,) + transfer.shape[1:], jnp.float32),
            pltpu.VMEM(vectors.shape, jnp.float32),
            pltpu.SemaphoreType.DMA((2 * slots + 3,)),
        ],
    )
    tops = [SLOT_BITS + places.low_bits + j for j in range(SLOT_BITS)]

    half = (slots // 2, rank, leaf)
    (sent,) = call(basis_first_kernel, [half], [target_t])
    first = places.flip_top(sent, 0)
    (sent,) = call(basis_second_kernel, [half], [target_t, first])
    second = places.flip_top(sent, 1)
    (basis_t,) = call(basis_settle_kernel, [basis_shape], [target_t, first, second])
    image_basis = places.reverse_low(basis_t)
    half = (slots // 2, SLOT_BITS * rank, lanes)
    (sent,) = call(functools.partial(tops_first_kernel, tops), [half], [transfer])
    first = places.flip_top(sent, 0)
    (sent,) = call(functools.partial(tops_second_kernel, tops), [half], [transfer, first])
    second = places.flip_top(sent, 1)

    *early_bits, last_bit = pair_bits
    weight_rows = diagonal_rows.shape[0]
    for bit in early_bits:
        partner = places.partner(coeffs, bit)
        cut = bit == early_bits[-1]
        rows = [len(piece) * rank for piece in FORWARD_PIECES]
        rows[0] += weight_rows
        coeffs, *others = call(
            functools.partial(cutting_pair_kernel if cut else pair_kernel, SLOT_BITS + bit, bit),
            [(n, vecs) for n in rows] if cut else [packed],
            [coeffs, partner, transfer],
        )
    messages = [coeffs] + others
    partners = [places.partner(message, last_bit) for message in messages]
    blocks = {}
    for j, piece in enumerate(FORWARD_PIECES):
        outs = call(
            functools.partial(last_pair_kernel, SLOT_BITS + last_bit, last_bit, piece),
            [node] * len(piece),
            [messages[j], partners[j], transfer],
        )
        blocks.update(zip(piece, outs))
    blocks = [blocks[k] for k in range(SLOTS)]
    if places.low_bits // 2 == 1:
        (weights,) = call(
            functools.partial(weights_kernel, last_bit, len(FORWARD_PIECES[0]) * rank),
            [diagonal_rows.shape],
            [diagonal_rows, partners[0]],
        )
    else:
        weights = places.reverse_low(diagonal).reshape(diagonal_rows.shape)

    square = (slots * rank, slots * rank)
    wide, middle = call(
        functools.partial(fold_kernel, tops),
        [square, square],
        [transfer, first, second, basis_t, weights],
        scratch=[
            pltpu.VMEM((SLOT_BITS, slots, rank, lanes), jnp.float32),
            pltpu.VMEM((slots, slots * rank, rank), jnp.float32),
        ],
    )

    blocks = places.across(blocks)
    back = places.across(call(middle_kernel, [node] * slots, [middle] + blocks))
    (coeffs,) = call(top_kernel, [nodes], [wide] + blocks)
    image_coeffs = places.reverse_low(coeffs)
    (forward_image,) = call(
        image_kernel,
        [vectors.shape],
        [image_basis, image_coeffs],
        out_specs=[ANY],
        scratch=rows_scratch,
    )

    pieces = []
    for piece in BACK_PIECES:
        shape = (len(piece), rank, vecs)
        sent, kept = call(
            functools.partial(first_part_kernel, SLOT_BITS + last_bit, last_bit, piece),
            [shape, shape],
            [transfer] + [back[k] for k in piece],
        )
        pieces += [kept, places.partner(sent, last_bit)]
    for bit in reversed(early_bits):
        sent, kept = call(
            functools.partial(
                joining_part_kernel if bit == early_bits[-1] else part_kernel, SLOT_BITS + bit, bit
            ),
            [nodes, nodes],
            [transfer] + pieces,
        )
        pieces = [kept, places.partner(sent, bit)]
    kept, arrived = pieces
    (adjoint,) = call(
        tail_kernel,
        [vectors.shape],
        [kept, arrived, transfer, source_t],
        out_specs=[ANY],
        scratch=rows_scratch,
    )
    return forward_image, adjoint


def solution(mesh):
    placed = (
        P(BOTH, None),
        P(BOTH),
        P(BOTH, None, None),
        P(None, BOTH, None, None),
        P(BOTH, None, None),
    )

    return jax.shard_map(
        body, mesh=mesh, in_specs=placed, out_specs=(P(BOTH, None), P(BOTH, None)), check_vma=False
    )
```

```python
import functools

import jax
import jax.numpy as jnp
from jax import lax
from jax.experimental import pallas as pl
from jax.experimental.pallas import tpu as pltpu
from jax.sharding import PartitionSpec as P


SLOT_BITS = 2
SLOTS = 2**SLOT_BITS
BOTH = ("row", "col")
CROSSING = sorted(range(1, SLOTS), key=lambda k: -k.bit_count())
FORWARD_PIECES = [CROSSING[: SLOTS // 2], CROSSING[SLOTS // 2 :] + [0]]
BACK_PIECES = [[0], CROSSING]
NN, TN, NT = ((1,), (0,)), ((0,), (0,)), ((1,), (1,))
VMEM = pl.BlockSpec(memory_space=pltpu.VMEM)
ANY = pl.BlockSpec(memory_space=pl.ANY)
HBM = pl.BlockSpec(memory_space=pltpu.HBM)


def reverse_bits(value, bits):
    out = 0
    for i in range(bits):
        out = out | ((value >> i) & 1) << (bits - 1 - i)
    return out


class Places:
    def __init__(self, slot_bits):
        self.devices = lax.axis_size("row") * lax.axis_size("col")
        self.low_bits = self.devices.bit_length() - 1 - slot_bits

    def permute(self, block, route):
        return lax.ppermute(block, BOTH, [(d, route(d)) for d in range(self.devices)])

    def partner(self, block, bit):
        return self.permute(block, lambda d: d ^ (1 << bit))

    def reverse_low(self, block):
        low = self.low_bits
        return self.permute(
            block, lambda d: (d >> low) << low | reverse_bits(d & (2**low - 1), low)
        )

    def flip_top(self, block, bit):
        return self.permute(block, lambda d: d ^ (1 << (self.low_bits + bit)))

    def across(self, blocks):
        return [
            b if k == 0 else self.permute(b, lambda d: d ^ (k << self.low_bits))
            for k, b in enumerate(blocks)
        ]


def place():
    return lax.axis_index("row") * lax.axis_size("col") + lax.axis_index("col")


def low_bits():
    return (lax.axis_size("row") * lax.axis_size("col")).bit_length() - 1 - SLOT_BITS


def met(k):
    return reverse_bits((place() >> low_bits()) ^ k, SLOT_BITS)


def bit_of_place(bit):
    return (place() >> bit) & 1


def is_upper(bit):
    return bit_of_place(bit) == 1


def top_pair():
    return bit_of_place(low_bits()), bit_of_place(low_bits() + 1)


def split(x):
    high = x.astype(jnp.bfloat16)
    return high, (x - high.astype(jnp.float32)).astype(jnp.bfloat16)


def product(a, b, dims):
    (ah, al), (bh, bl) = split(a), split(b)

    def dot(x, y):
        return lax.dot_general(x, y, (dims, ((), ())), preferred_element_type=jnp.float32)

    return dot(ah, bh) + (dot(ah, bl) + dot(al, bh))


def call(
    kernel, outs, operands, specs=None, out_specs=None, scratch=(), flops=1 << 24, kind=jnp.float32
):
    shapes = [jax.ShapeDtypeStruct(s, kind) for s in outs]
    return pl.pallas_call(
        kernel,
        out_shape=shapes,
        in_specs=specs or [VMEM] * len(operands),
        out_specs=out_specs or [VMEM] * len(outs),
        scratch_shapes=list(scratch),
        compiler_params=pltpu.CompilerParams(vmem_limit_bytes=8 << 20),
        cost_estimate=pl.CostEstimate(flops=flops, bytes_accessed=1 << 19, transcendentals=0),
    )(*operands)


def store(out, nodes, weights):
    rank = nodes[0].shape[0]
    for at, node in enumerate(nodes):
        out[at * rank : (at + 1) * rank] = node
    if weights is not None:
        out[len(nodes) * rank :] = weights


def head_kernel(
    vectors_in,
    basis_in,
    transfer_in,
    target_in,
    diagonal_in,
    out,
    basis,
    target,
    diagonal,
    transfer,
    vectors,
    sems,
):
    leaf = basis.shape[2]
    copies = []

    def fetch(source, to):
        copies.append(pltpu.make_async_copy(source, to, sems.at[len(copies)]))
        copies[-1].start()
        return copies[-1]

    first = fetch(transfer_in.at[pl.ds(0, SLOT_BITS)], transfer)
    slots = []
    for s in range(SLOTS):
        rows = pl.ds(s * leaf, leaf)
        slots.append(
            (fetch(basis_in.at[s], basis.at[s]), fetch(vectors_in.at[rows], vectors.at[rows]))
        )
    weights = fetch(diagonal_in, diagonal)
    later = fetch(target_in, target)
    first.wait()
    rank = basis.shape[1]
    blocks, sources = compose(transfer, list(range(SLOT_BITS)), rank)
    levels = jnp.concatenate(blocks, axis=0)
    c = []
    for s in range(SLOTS):
        for copy in slots[s]:
            copy.wait()
        c.append(product(basis[s], vectors[s * leaf : (s + 1) * leaf], NN))
    out_rows = product(levels, jnp.concatenate([c[s] for s in sources[0]], axis=0), NN)
    c = [out_rows[s * rank : (s + 1) * rank] for s in range(SLOTS)]
    weights.wait()
    store(out, c, diagonal[...])
    later.wait()


def join(level, bit, s, at, own, partner, transfer):
    rank = transfer.shape[2]
    rows = pl.ds(pl.multiple_of(at * rank, rank), rank)
    upper = is_upper(bit)
    lower_half = jnp.where(upper, partner[rows], own[rows])
    upper_half = jnp.where(upper, own[rows], partner[rows])
    return product(transfer[level, s], jnp.concatenate([lower_half, upper_half], axis=0), NN)


def weights_of(bit, own, partner, rank):
    return (partner if bit == 0 else own)[SLOTS * rank :]


def pair_kernel(level, bit, own, partner, transfer, out):
    nodes = [join(level, bit, s, s, own, partner, transfer) for s in range(SLOTS)]
    store(out, nodes, weights_of(bit, own, partner, transfer.shape[2]))


def cutting_pair_kernel(level, bit, own, partner, transfer, *outs):
    for j, piece in enumerate(FORWARD_PIECES):
        nodes = [join(level, bit, met(k), met(k), own, partner, transfer) for k in piece]
        weights = weights_of(bit, own, partner, transfer.shape[2]) if j == 0 else None
        store(outs[j], nodes, weights)


def last_pair_kernel(level, bit, piece, own, partner, transfer, *outs):
    for at, k in enumerate(piece):
        outs[at][...] = join(level, bit, met(k), at, own, partner, transfer)


def weights_kernel(bit, rows, diagonal, partner, out):
    same = bit_of_place(0) == bit_of_place(bit)
    out[...] = jnp.where(same, diagonal[...], partner[rows:])


def tops_of(transfer, levels, s):
    return jnp.concatenate([transfer[level, s] for level in levels], axis=0)


def first_step(read, out):
    x, _ = top_pair()
    for v in range(2):
        out[v] = read((x ^ 1) << 1 | v)


def second_step(read, first, out):
    x, y = top_pair()
    out[x] = read(x << 1 | (y ^ 1))
    out[x ^ 1] = first[y ^ 1]


def settle(read, first, second, write):
    x, y = top_pair()
    write(x << 1 | y, read(x << 1 | y))
    write((x ^ 1) << 1 | y, first[y])
    for w in range(2):
        write(w << 1 | (y ^ 1), second[w])


def basis_first_kernel(basis, out):
    first_step(lambda s: basis[s], out)


def basis_second_kernel(basis, first, out):
    second_step(lambda s: basis[s], first, out)


def basis_settle_kernel(basis, first, second, out):
    def write(s, block):
        out[s] = block

    settle(lambda s: basis[s], first, second, write)


def tops_first_kernel(levels, transfer, out):
    first_step(lambda s: tops_of(transfer, levels, s), out)


def tops_second_kernel(levels, transfer, first, out):
    second_step(lambda s: tops_of(transfer, levels, s), first, out)


def compose(levels, bits, rank):
    blocks = [levels[0, s] for s in range(SLOTS)]
    sources = [[s & ~(1 << bits[0]), s | 1 << bits[0]] for s in range(SLOTS)]
    for j in range(1, SLOT_BITS):
        bit = 1 << bits[j]
        old, old_sources = blocks, sources
        blocks, sources = [], []
        for s in range(SLOTS):
            halves = [
                product(levels[j, s][:, e * rank : (e + 1) * rank], old[q], NN)
                for e, q in enumerate((s & ~bit, s | bit))
            ]
            blocks.append(jnp.concatenate(halves, axis=1))
            sources.append(old_sources[s & ~bit] + old_sources[s | bit])
    return blocks, sources


def fold_kernel(levels, transfer, first, second, basis, weights, wide, middle, tops, columns):
    rank = basis.shape[1]

    def write(s, block):
        for j in range(SLOT_BITS):
            tops[j, s] = block[j * rank : (j + 1) * rank]

    settle(lambda s: tops_of(transfer, levels, s), first, second, write)
    blocks, sources = compose(tops, list(reversed(range(SLOT_BITS))), rank)
    for s in range(SLOTS):
        for at, source in enumerate(sources[s]):
            columns[source, s * rank : (s + 1) * rank] = blocks[s][:, at * rank : (at + 1) * rank]
    ordered = jnp.concatenate([columns[met(k)] for k in range(SLOTS)], axis=1)
    wide[...] = ordered
    inner = []
    for s in range(SLOTS):
        rows = weights.shape[0] // SLOTS
        weight = jnp.concatenate([weights[j : j + 1] for j in range(s * rows, (s + 1) * rows)], axis=1)
        gram = product(basis[s] * weight, basis[s], NT)
        inner.append(product(gram, ordered[s * rank : (s + 1) * rank], NN))
    middle[...] = product(ordered, jnp.concatenate(inner, axis=0), TN)


def middle_kernel(middle, *refs):
    blocks, outs = refs[:SLOTS], refs[SLOTS:]
    rank = blocks[0].shape[0]
    out = product(middle[...], jnp.concatenate([b[...] for b in blocks], axis=0), NN)
    for k in range(SLOTS):
        outs[k][...] = out[k * rank : (k + 1) * rank]


def top_kernel(wide, *refs):
    blocks, out = refs[:SLOTS], refs[SLOTS]
    rank = blocks[0].shape[0]
    rows = product(wide[...], jnp.concatenate([b[...] for b in blocks], axis=0), NN)
    for s in range(SLOTS):
        out[s] = rows[s * rank : (s + 1) * rank]


def part(level, bit, s, at, block, transfer, sent, kept):
    upper = is_upper(bit)
    out = product(transfer[level, s], block, TN)
    rank = sent.shape[1]
    sent[at] = jnp.where(upper, out[:rank], out[rank:])
    kept[at] = jnp.where(upper, out[rank:], out[:rank])


def first_part_kernel(level, bit, piece, transfer, *refs):
    sent, kept = refs[len(piece) :]
    for at, k in enumerate(piece):
        part(level, bit, met(k), at, refs[at][...], transfer, sent, kept)


def joining_part_kernel(level, bit, transfer, *refs):
    sent, kept = refs[-2:]
    for j, piece in enumerate(BACK_PIECES):
        kept_in, arrived = refs[2 * j : 2 * j + 2]
        for at, k in enumerate(piece):
            s = met(k)
            part(level, bit, s, s, kept_in[at] + arrived[at], transfer, sent, kept)


def part_kernel(level, bit, transfer, kept_in, arrived, sent, kept):
    for s in range(SLOTS):
        part(level, bit, s, s, kept_in[s] + arrived[s], transfer, sent, kept)


def write_rows(rows, out, buffer, sems):
    copies = []
    for s in range(SLOTS):
        leaf = buffer.shape[1]
        buffer[s] = rows(s)
        copies.append(
            pltpu.make_async_copy(buffer.at[s], out.at[pl.ds(s * leaf, leaf)], sems.at[s])
        )
        copies[-1].start()
    for copy in copies:
        copy.wait()


def source_fold_kernel(transfer, basis, high, low):
    rank = basis.shape[1]
    blocks, sources = compose(transfer, list(range(SLOT_BITS)), rank)
    rows = jnp.concatenate(blocks, axis=0)
    for at, source in enumerate(sources[0]):
        through = product(rows[:, at * rank : (at + 1) * rank], basis[source], NN)
        high[source], low[source] = split(through.T)


def tail_kernel(kept, arrived, high, low, out, buffer, sems):
    b = jnp.concatenate([kept[s] + arrived[s] for s in range(SLOTS)], axis=0)
    bh, bl = split(b)

    def dot(x, y):
        return lax.dot_general(x, y, (NN, ((), ())), preferred_element_type=jnp.float32)

    write_rows(
        lambda s: dot(high[s], bh) + (dot(high[s], bl) + dot(low[s], bh)), out, buffer, sems
    )


def image_kernel(basis, coeffs, out, buffer, sems):
    write_rows(lambda s: product(basis[s], coeffs[s], TN), out, buffer, sems)


def body(vectors, diagonal, source_basis, transfer, target_basis):
    slots, leaf, rank = source_basis.shape
    vecs = vectors.shape[-1]
    places = Places(SLOT_BITS)
    pair_bits = list(range(places.low_bits))
    nodes, node = (slots, rank, vecs), (rank, vecs)
    basis_shape = (slots, rank, leaf)
    rows_scratch = [pltpu.VMEM((slots, leaf, vecs), jnp.float32), pltpu.SemaphoreType.DMA((slots,))]
    source_t = jnp.swapaxes(source_basis, 1, 2)
    target_t = jnp.swapaxes(target_basis, 1, 2)
    lanes = transfer.shape[3]
    diagonal_rows = diagonal.reshape(-1, lanes)
    packed = (slots * rank + diagonal_rows.shape[0], vecs)
    coeffs, source_t, target_t, diagonal_rows = call(
        head_kernel,
        [packed, basis_shape, basis_shape, diagonal_rows.shape],
        [
            pltpu.with_memory_space_constraint(x, pltpu.HBM)
            for x in (vectors, source_t, transfer, target_t, diagonal_rows)
        ],
        [HBM] * 5,
        scratch=[
            pltpu.VMEM((SLOT_BITS,) + transfer.shape[1:], jnp.float32),
            pltpu.VMEM(vectors.shape, jnp.float32),
            pltpu.SemaphoreType.DMA((2 * slots + 3,)),
        ],
    )
    tops = [SLOT_BITS + places.low_bits + j for j in range(SLOT_BITS)]

    half = (slots // 2, rank, leaf)
    (sent,) = call(basis_first_kernel, [half], [target_t])
    first = places.flip_top(sent, 0)
    (sent,) = call(basis_second_kernel, [half], [target_t, first])
    second = places.flip_top(sent, 1)
    (basis_t,) = call(basis_settle_kernel, [basis_shape], [target_t, first, second])
    image_basis = places.reverse_low(basis_t)
    half = (slots // 2, SLOT_BITS * rank, lanes)
    (sent,) = call(functools.partial(tops_first_kernel, tops), [half], [transfer])
    first = places.flip_top(sent, 0)
    (sent,) = call(functools.partial(tops_second_kernel, tops), [half], [transfer, first])
    second = places.flip_top(sent, 1)

    *early_bits, last_bit = pair_bits
    weight_rows = diagonal_rows.shape[0]
    for bit in early_bits:
        partner = places.partner(coeffs, bit)
        cut = bit == early_bits[-1]
        rows = [len(piece) * rank for piece in FORWARD_PIECES]
        rows[0] += weight_rows
        coeffs, *others = call(
            functools.partial(cutting_pair_kernel if cut else pair_kernel, SLOT_BITS + bit, bit),
            [(n, vecs) for n in rows] if cut else [packed],
            [coeffs, partner, transfer],
        )
    messages = [coeffs] + others
    partners = [places.partner(message, last_bit) for message in messages]
    blocks = {}
    for j, piece in enumerate(FORWARD_PIECES):
        outs = call(
            functools.partial(last_pair_kernel, SLOT_BITS + last_bit, last_bit, piece),
            [node] * len(piece),
            [messages[j], partners[j], transfer],
        )
        blocks.update(zip(piece, outs))
    blocks = [blocks[k] for k in range(SLOTS)]
    if places.low_bits // 2 == 1:
        (weights,) = call(
            functools.partial(weights_kernel, last_bit, len(FORWARD_PIECES[0]) * rank),
            [diagonal_rows.shape],
            [diagonal_rows, partners[0]],
        )
    else:
        weights = places.reverse_low(diagonal).reshape(diagonal_rows.shape)

    square = (slots * rank, slots * rank)
    wide, middle = call(
        functools.partial(fold_kernel, tops),
        [square, square],
        [transfer, first, second, basis_t, weights],
        scratch=[
            pltpu.VMEM((SLOT_BITS, slots, rank, lanes), jnp.float32),
            pltpu.VMEM((slots, slots * rank, rank), jnp.float32),
        ],
    )

    blocks = places.across(blocks)
    back = places.across(call(middle_kernel, [node] * slots, [middle] + blocks))
    (coeffs,) = call(top_kernel, [nodes], [wide] + blocks)
    image_coeffs = places.reverse_low(coeffs)
    (forward_image,) = call(
        image_kernel,
        [vectors.shape],
        [image_basis, image_coeffs],
        out_specs=[ANY],
        scratch=rows_scratch,
    )

    source_fold = call(
        source_fold_kernel,
        [(slots, leaf, slots * rank)] * 2,
        [transfer, source_t],
        kind=jnp.bfloat16,
    )
    pieces = []
    for piece in BACK_PIECES:
        shape = (len(piece), rank, vecs)
        sent, kept = call(
            functools.partial(first_part_kernel, SLOT_BITS + last_bit, last_bit, piece),
            [shape, shape],
            [transfer] + [back[k] for k in piece],
        )
        pieces += [kept, places.partner(sent, last_bit)]
    for bit in reversed(early_bits):
        sent, kept = call(
            functools.partial(
                joining_part_kernel if bit == early_bits[-1] else part_kernel, SLOT_BITS + bit, bit
            ),
            [nodes, nodes],
            [transfer] + pieces,
        )
        pieces = [kept, places.partner(sent, bit)]
    kept, arrived = pieces
    (adjoint,) = call(
        tail_kernel,
        [vectors.shape],
        [kept, arrived, *source_fold],
        out_specs=[ANY],
        scratch=rows_scratch,
    )
    return forward_image, adjoint


def solution(mesh):
    placed = (
        P(BOTH, None),
        P(BOTH),
        P(BOTH, None, None),
        P(None, BOTH, None, None),
        P(BOTH, None, None),
    )

    return jax.shard_map(
        body, mesh=mesh, in_specs=placed, out_specs=(P(BOTH, None), P(BOTH, None)), check_vma=False
    )
```

```python
import functools

import jax
import jax.numpy as jnp
from jax import lax
from jax.experimental import pallas as pl
from jax.experimental.pallas import tpu as pltpu
from jax.sharding import PartitionSpec as P


SLOT_BITS = 2
SLOTS = 2**SLOT_BITS
BOTH = ("row", "col")
CROSSING = sorted(range(1, SLOTS), key=lambda k: -k.bit_count())
FORWARD_PIECES = [CROSSING[: SLOTS // 2], CROSSING[SLOTS // 2 :] + [0]]
BACK_PIECES = [[0], CROSSING]
NN, TN, NT = ((1,), (0,)), ((0,), (0,)), ((1,), (1,))
VMEM = pl.BlockSpec(memory_space=pltpu.VMEM)
ANY = pl.BlockSpec(memory_space=pl.ANY)
HBM = pl.BlockSpec(memory_space=pltpu.HBM)


def reverse_bits(value, bits):
    out = 0
    for i in range(bits):
        out = out | ((value >> i) & 1) << (bits - 1 - i)
    return out


class Places:
    def __init__(self, slot_bits):
        self.devices = lax.axis_size("row") * lax.axis_size("col")
        self.low_bits = self.devices.bit_length() - 1 - slot_bits

    def permute(self, block, route):
        return lax.ppermute(block, BOTH, [(d, route(d)) for d in range(self.devices)])

    def partner(self, block, bit):
        return self.permute(block, lambda d: d ^ (1 << bit))

    def reverse_low(self, block):
        low = self.low_bits
        return self.permute(
            block, lambda d: (d >> low) << low | reverse_bits(d & (2**low - 1), low)
        )

    def flip_top(self, block, bit):
        return self.permute(block, lambda d: d ^ (1 << (self.low_bits + bit)))

    def across(self, blocks):
        return [
            b if k == 0 else self.permute(b, lambda d: d ^ (k << self.low_bits))
            for k, b in enumerate(blocks)
        ]


def place():
    return lax.axis_index("row") * lax.axis_size("col") + lax.axis_index("col")


def low_bits():
    return (lax.axis_size("row") * lax.axis_size("col")).bit_length() - 1 - SLOT_BITS


def met(k):
    return reverse_bits((place() >> low_bits()) ^ k, SLOT_BITS)


def bit_of_place(bit):
    return (place() >> bit) & 1


def is_upper(bit):
    return bit_of_place(bit) == 1


def top_pair():
    return bit_of_place(low_bits()), bit_of_place(low_bits() + 1)


def split(x):
    high = x.astype(jnp.bfloat16)
    return high, (x - high.astype(jnp.float32)).astype(jnp.bfloat16)


def product(a, b, dims):
    (ah, al), (bh, bl) = split(a), split(b)

    def dot(x, y):
        return lax.dot_general(x, y, (dims, ((), ())), preferred_element_type=jnp.float32)

    return dot(ah, bh) + (dot(ah, bl) + dot(al, bh))


def call(
    kernel, outs, operands, specs=None, out_specs=None, scratch=(), flops=1 << 24, kind=jnp.float32
):
    shapes = [jax.ShapeDtypeStruct(s, kind) for s in outs]
    return pl.pallas_call(
        kernel,
        out_shape=shapes,
        in_specs=specs or [VMEM] * len(operands),
        out_specs=out_specs or [VMEM] * len(outs),
        scratch_shapes=list(scratch),
        compiler_params=pltpu.CompilerParams(vmem_limit_bytes=8 << 20),
        cost_estimate=pl.CostEstimate(flops=flops, bytes_accessed=1 << 19, transcendentals=0),
    )(*operands)


def pairs(bit):
    return [(s, s | 1 << bit) for s in range(SLOTS) if not s >> bit & 1]


def store(out, nodes, weights):
    rank = nodes[0].shape[0]
    for at, node in enumerate(nodes):
        out[at * rank : (at + 1) * rank] = node
    if weights is not None:
        out[len(nodes) * rank :] = weights


def head_kernel(
    vectors_in,
    basis_in,
    transfer_in,
    diagonal_in,
    out,
    basis,
    diagonal,
    transfer,
    vectors,
    sems,
):
    leaf = basis.shape[2]
    copies = []

    def fetch(source, to):
        copies.append(pltpu.make_async_copy(source, to, sems.at[len(copies)]))
        copies[-1].start()
        return copies[-1]

    slots = []
    for s in range(SLOTS):
        rows = pl.ds(s * leaf, leaf)
        slots.append(
            (fetch(basis_in.at[s], basis.at[s]), fetch(vectors_in.at[rows], vectors.at[rows]))
        )
    first = fetch(transfer_in.at[pl.ds(0, SLOT_BITS)], transfer)
    weights = fetch(diagonal_in, diagonal)
    c = []
    for s in range(SLOTS):
        for copy in slots[s]:
            copy.wait()
        c.append(product(basis[s], vectors[s * leaf : (s + 1) * leaf], NN))
    first.wait()
    for level in range(SLOT_BITS):
        for low, high in pairs(level):
            both = jnp.concatenate([c[low], c[high]], axis=0)
            c[low] = product(transfer[level, low], both, NN)
            c[high] = product(transfer[level, high], both, NN)
    weights.wait()
    store(out, c, diagonal[...])


def join(level, bit, s, at, own, partner, transfer):
    rank = transfer.shape[2]
    rows = pl.ds(pl.multiple_of(at * rank, rank), rank)
    upper = is_upper(bit)
    lower_half = jnp.where(upper, partner[rows], own[rows])
    upper_half = jnp.where(upper, own[rows], partner[rows])
    return product(transfer[level, s], jnp.concatenate([lower_half, upper_half], axis=0), NN)


def weights_of(bit, own, partner, rank):
    return (partner if bit == 0 else own)[SLOTS * rank :]


def pair_kernel(level, bit, own, partner, transfer, out):
    nodes = [join(level, bit, s, s, own, partner, transfer) for s in range(SLOTS)]
    store(out, nodes, weights_of(bit, own, partner, transfer.shape[2]))


def cutting_pair_kernel(level, bit, own, partner, transfer, *outs):
    for j, piece in enumerate(FORWARD_PIECES):
        nodes = [join(level, bit, met(k), met(k), own, partner, transfer) for k in piece]
        weights = weights_of(bit, own, partner, transfer.shape[2]) if j == 0 else None
        store(outs[j], nodes, weights)


def last_pair_kernel(level, bit, piece, own, partner, transfer, *outs):
    for at, k in enumerate(piece):
        outs[at][...] = join(level, bit, met(k), at, own, partner, transfer)


def weights_kernel(bit, rows, diagonal, partner, out):
    same = bit_of_place(0) == bit_of_place(bit)
    out[...] = jnp.where(same, diagonal[...], partner[rows:])


def tops_of(transfer, levels, s):
    return jnp.concatenate([transfer[level, s] for level in levels], axis=0)


def first_step(read, out):
    x, _ = top_pair()
    for v in range(2):
        out[v] = read((x ^ 1) << 1 | v)


def second_step(read, first, out):
    x, y = top_pair()
    out[x] = read(x << 1 | (y ^ 1))
    out[x ^ 1] = first[y ^ 1]


def settle(read, first, second, write):
    x, y = top_pair()
    write(x << 1 | y, read(x << 1 | y))
    write((x ^ 1) << 1 | y, first[y])
    for w in range(2):
        write(w << 1 | (y ^ 1), second[w])


def basis_first_kernel(basis, out):
    first_step(lambda s: basis[s], out)


def basis_second_kernel(basis, first, out):
    second_step(lambda s: basis[s], first, out)


def basis_settle_kernel(basis, first, second, out):
    def write(s, block):
        out[s] = block

    settle(lambda s: basis[s], first, second, write)


def tops_first_kernel(levels, transfer, out):
    first_step(lambda s: tops_of(transfer, levels, s), out)


def tops_second_kernel(levels, transfer, first, out):
    second_step(lambda s: tops_of(transfer, levels, s), first, out)


def compose(levels, bits, rank):
    blocks = [levels[0, s] for s in range(SLOTS)]
    sources = [[s & ~(1 << bits[0]), s | 1 << bits[0]] for s in range(SLOTS)]
    for j in range(1, SLOT_BITS):
        bit = 1 << bits[j]
        old, old_sources = blocks, sources
        blocks, sources = [], []
        for s in range(SLOTS):
            halves = [
                product(levels[j, s][:, e * rank : (e + 1) * rank], old[q], NN)
                for e, q in enumerate((s & ~bit, s | bit))
            ]
            blocks.append(jnp.concatenate(halves, axis=1))
            sources.append(old_sources[s & ~bit] + old_sources[s | bit])
    return blocks, sources


def fold_kernel(levels, transfer, first, second, basis, weights, wide, middle, tops, columns):
    rank = basis.shape[1]

    def write(s, block):
        for j in range(SLOT_BITS):
            tops[j, s] = block[j * rank : (j + 1) * rank]

    settle(lambda s: tops_of(transfer, levels, s), first, second, write)
    blocks, sources = compose(tops, list(reversed(range(SLOT_BITS))), rank)
    for s in range(SLOTS):
        for at, source in enumerate(sources[s]):
            columns[source, s * rank : (s + 1) * rank] = blocks[s][:, at * rank : (at + 1) * rank]
    ordered = jnp.concatenate([columns[met(k)] for k in range(SLOTS)], axis=1)
    wide[...] = ordered
    inner = []
    for s in range(SLOTS):
        rows = weights.shape[0] // SLOTS
        weight = jnp.concatenate([weights[j : j + 1] for j in range(s * rows, (s + 1) * rows)], axis=1)
        gram = product(basis[s] * weight, basis[s], NT)
        inner.append(product(gram, ordered[s * rank : (s + 1) * rank], NN))
    middle[...] = product(ordered, jnp.concatenate(inner, axis=0), TN)


def middle_kernel(middle, *refs):
    blocks, outs = refs[:SLOTS], refs[SLOTS:]
    rank = blocks[0].shape[0]
    out = product(middle[...], jnp.concatenate([b[...] for b in blocks], axis=0), NN)
    for k in range(SLOTS):
        outs[k][...] = out[k * rank : (k + 1) * rank]


def top_kernel(wide, *refs):
    blocks, out = refs[:SLOTS], refs[SLOTS]
    rank = blocks[0].shape[0]
    rows = product(wide[...], jnp.concatenate([b[...] for b in blocks], axis=0), NN)
    for s in range(SLOTS):
        out[s] = rows[s * rank : (s + 1) * rank]


def part(level, bit, s, at, block, transfer, sent, kept):
    upper = is_upper(bit)
    out = product(transfer[level, s], block, TN)
    rank = sent.shape[1]
    sent[at] = jnp.where(upper, out[:rank], out[rank:])
    kept[at] = jnp.where(upper, out[rank:], out[:rank])


def first_part_kernel(level, bit, piece, transfer, *refs):
    sent, kept = refs[len(piece) :]
    for at, k in enumerate(piece):
        part(level, bit, met(k), at, refs[at][...], transfer, sent, kept)


def joining_part_kernel(level, bit, transfer, *refs):
    sent, kept = refs[-2:]
    for j, piece in enumerate(BACK_PIECES):
        kept_in, arrived = refs[2 * j : 2 * j + 2]
        for at, k in enumerate(piece):
            s = met(k)
            part(level, bit, s, s, kept_in[at] + arrived[at], transfer, sent, kept)


def part_kernel(level, bit, transfer, kept_in, arrived, sent, kept):
    for s in range(SLOTS):
        part(level, bit, s, s, kept_in[s] + arrived[s], transfer, sent, kept)


def write_rows(rows, out, buffer, sems):
    copies = []
    for s in range(SLOTS):
        leaf = buffer.shape[1]
        buffer[s] = rows(s)
        copies.append(
            pltpu.make_async_copy(buffer.at[s], out.at[pl.ds(s * leaf, leaf)], sems.at[s])
        )
        copies[-1].start()
    for copy in copies:
        copy.wait()


def source_fold_kernel(transfer, basis, high, low):
    rank = basis.shape[1]
    blocks, sources = compose(transfer, list(range(SLOT_BITS)), rank)
    rows = jnp.concatenate(blocks, axis=0)
    for at, source in enumerate(sources[0]):
        through = product(rows[:, at * rank : (at + 1) * rank], basis[source], NN)
        high[source], low[source] = split(through.T)


def tail_kernel(kept, arrived, high, low, out, buffer, sems):
    b = jnp.concatenate([kept[s] + arrived[s] for s in range(SLOTS)], axis=0)
    bh, bl = split(b)

    def dot(x, y):
        return lax.dot_general(x, y, (NN, ((), ())), preferred_element_type=jnp.float32)

    write_rows(
        lambda s: dot(high[s], bh) + (dot(high[s], bl) + dot(low[s], bh)), out, buffer, sems
    )


def image_kernel(basis, coeffs, out, buffer, sems):
    write_rows(lambda s: product(basis[s], coeffs[s], TN), out, buffer, sems)


def body(vectors, diagonal, source_basis, transfer, target_basis):
    slots, leaf, rank = source_basis.shape
    vecs = vectors.shape[-1]
    places = Places(SLOT_BITS)
    pair_bits = list(range(places.low_bits))
    nodes, node = (slots, rank, vecs), (rank, vecs)
    basis_shape = (slots, rank, leaf)
    rows_scratch = [pltpu.VMEM((slots, leaf, vecs), jnp.float32), pltpu.SemaphoreType.DMA((slots,))]
    source_t = jnp.swapaxes(source_basis, 1, 2)
    target_t = jnp.swapaxes(target_basis, 1, 2)
    lanes = transfer.shape[3]
    diagonal_rows = diagonal.reshape(-1, lanes)
    packed = (slots * rank + diagonal_rows.shape[0], vecs)
    coeffs, source_t, diagonal_rows = call(
        head_kernel,
        [packed, basis_shape, diagonal_rows.shape],
        [
            pltpu.with_memory_space_constraint(x, pltpu.HBM)
            for x in (vectors, source_t, transfer, diagonal_rows)
        ],
        [HBM] * 4,
        scratch=[
            pltpu.VMEM((SLOT_BITS,) + transfer.shape[1:], jnp.float32),
            pltpu.VMEM(vectors.shape, jnp.float32),
            pltpu.SemaphoreType.DMA((2 * slots + 2,)),
        ],
    )
    tops = [SLOT_BITS + places.low_bits + j for j in range(SLOT_BITS)]

    half = (slots // 2, rank, leaf)
    (sent,) = call(basis_first_kernel, [half], [target_t])
    first = places.flip_top(sent, 0)
    (sent,) = call(basis_second_kernel, [half], [target_t, first])
    second = places.flip_top(sent, 1)
    (basis_t,) = call(basis_settle_kernel, [basis_shape], [target_t, first, second])
    image_basis = places.reverse_low(basis_t)
    half = (slots // 2, SLOT_BITS * rank, lanes)
    (sent,) = call(functools.partial(tops_first_kernel, tops), [half], [transfer])
    first = places.flip_top(sent, 0)
    (sent,) = call(functools.partial(tops_second_kernel, tops), [half], [transfer, first])
    second = places.flip_top(sent, 1)

    *early_bits, last_bit = pair_bits
    weight_rows = diagonal_rows.shape[0]
    for bit in early_bits:
        partner = places.partner(coeffs, bit)
        cut = bit == early_bits[-1]
        rows = [len(piece) * rank for piece in FORWARD_PIECES]
        rows[0] += weight_rows
        coeffs, *others = call(
            functools.partial(cutting_pair_kernel if cut else pair_kernel, SLOT_BITS + bit, bit),
            [(n, vecs) for n in rows] if cut else [packed],
            [coeffs, partner, transfer],
        )
    messages = [coeffs] + others
    partners = [places.partner(message, last_bit) for message in messages]
    blocks = {}
    for j, piece in enumerate(FORWARD_PIECES):
        outs = call(
            functools.partial(last_pair_kernel, SLOT_BITS + last_bit, last_bit, piece),
            [node] * len(piece),
            [messages[j], partners[j], transfer],
        )
        blocks.update(zip(piece, outs))
    blocks = [blocks[k] for k in range(SLOTS)]
    if places.low_bits // 2 == 1:
        (weights,) = call(
            functools.partial(weights_kernel, last_bit, len(FORWARD_PIECES[0]) * rank),
            [diagonal_rows.shape],
            [diagonal_rows, partners[0]],
        )
    else:
        weights = places.reverse_low(diagonal).reshape(diagonal_rows.shape)

    square = (slots * rank, slots * rank)
    wide, middle = call(
        functools.partial(fold_kernel, tops),
        [square, square],
        [transfer, first, second, basis_t, weights],
        scratch=[
            pltpu.VMEM((SLOT_BITS, slots, rank, lanes), jnp.float32),
            pltpu.VMEM((slots, slots * rank, rank), jnp.float32),
        ],
    )

    blocks = places.across(blocks)
    back = places.across(call(middle_kernel, [node] * slots, [middle] + blocks))
    (coeffs,) = call(top_kernel, [nodes], [wide] + blocks)
    image_coeffs = places.reverse_low(coeffs)
    (forward_image,) = call(
        image_kernel,
        [vectors.shape],
        [image_basis, image_coeffs],
        out_specs=[ANY],
        scratch=rows_scratch,
    )

    source_fold = call(
        source_fold_kernel,
        [(slots, leaf, slots * rank)] * 2,
        [transfer, source_t],
        kind=jnp.bfloat16,
    )
    pieces = []
    for piece in BACK_PIECES:
        shape = (len(piece), rank, vecs)
        sent, kept = call(
            functools.partial(first_part_kernel, SLOT_BITS + last_bit, last_bit, piece),
            [shape, shape],
            [transfer] + [back[k] for k in piece],
        )
        pieces += [kept, places.partner(sent, last_bit)]
    for bit in reversed(early_bits):
        sent, kept = call(
            functools.partial(
                joining_part_kernel if bit == early_bits[-1] else part_kernel, SLOT_BITS + bit, bit
            ),
            [nodes, nodes],
            [transfer] + pieces,
        )
        pieces = [kept, places.partner(sent, bit)]
    kept, arrived = pieces
    (adjoint,) = call(
        tail_kernel,
        [vectors.shape],
        [kept, arrived, *source_fold],
        out_specs=[ANY],
        scratch=rows_scratch,
    )
    return forward_image, adjoint


def solution(mesh):
    placed = (
        P(BOTH, None),
        P(BOTH),
        P(BOTH, None, None),
        P(None, BOTH, None, None),
        P(BOTH, None, None),
    )

    return jax.shard_map(
        body, mesh=mesh, in_specs=placed, out_specs=(P(BOTH, None), P(BOTH, None)), check_vma=False
    )
```

```python
import functools

import jax
import jax.numpy as jnp
from jax import lax
from jax.experimental import pallas as pl
from jax.experimental.pallas import tpu as pltpu
from jax.sharding import PartitionSpec as P


SLOT_BITS = 2
SLOTS = 2**SLOT_BITS
BOTH = ("row", "col")
CROSSING = sorted(range(1, SLOTS), key=lambda k: -k.bit_count())
FORWARD_PIECES = [CROSSING[: SLOTS // 2], CROSSING[SLOTS // 2 :] + [0]]
BACK_PIECES = [[0] + CROSSING[:1], CROSSING[1:]]
NN, TN, NT = ((1,), (0,)), ((0,), (0,)), ((1,), (1,))
VMEM = pl.BlockSpec(memory_space=pltpu.VMEM)
ANY = pl.BlockSpec(memory_space=pl.ANY)
HBM = pl.BlockSpec(memory_space=pltpu.HBM)


def reverse_bits(value, bits):
    out = 0
    for i in range(bits):
        out = out | ((value >> i) & 1) << (bits - 1 - i)
    return out


class Places:
    def __init__(self, slot_bits):
        self.devices = lax.axis_size("row") * lax.axis_size("col")
        self.low_bits = self.devices.bit_length() - 1 - slot_bits

    def permute(self, block, route):
        return lax.ppermute(block, BOTH, [(d, route(d)) for d in range(self.devices)])

    def partner(self, block, bit):
        return self.permute(block, lambda d: d ^ (1 << bit))

    def reverse_low(self, block):
        low = self.low_bits
        return self.permute(
            block, lambda d: (d >> low) << low | reverse_bits(d & (2**low - 1), low)
        )

    def flip_top(self, block, bit):
        return self.permute(block, lambda d: d ^ (1 << (self.low_bits + bit)))

    def across(self, blocks):
        return [
            b if k == 0 else self.permute(b, lambda d: d ^ (k << self.low_bits))
            for k, b in enumerate(blocks)
        ]


def place():
    return lax.axis_index("row") * lax.axis_size("col") + lax.axis_index("col")


def low_bits():
    return (lax.axis_size("row") * lax.axis_size("col")).bit_length() - 1 - SLOT_BITS


def met(k):
    return reverse_bits((place() >> low_bits()) ^ k, SLOT_BITS)


def bit_of_place(bit):
    return (place() >> bit) & 1


def is_upper(bit):
    return bit_of_place(bit) == 1


def top_pair():
    return bit_of_place(low_bits()), bit_of_place(low_bits() + 1)


def split(x):
    high = x.astype(jnp.bfloat16)
    return high, (x - high.astype(jnp.float32)).astype(jnp.bfloat16)


def product(a, b, dims):
    (ah, al), (bh, bl) = split(a), split(b)

    def dot(x, y):
        return lax.dot_general(x, y, (dims, ((), ())), preferred_element_type=jnp.float32)

    return dot(ah, bh) + (dot(ah, bl) + dot(al, bh))


def call(
    kernel, outs, operands, specs=None, out_specs=None, scratch=(), flops=1 << 24, kind=jnp.float32
):
    shapes = [jax.ShapeDtypeStruct(s, kind) for s in outs]
    return pl.pallas_call(
        kernel,
        out_shape=shapes,
        in_specs=specs or [VMEM] * len(operands),
        out_specs=out_specs or [VMEM] * len(outs),
        scratch_shapes=list(scratch),
        compiler_params=pltpu.CompilerParams(vmem_limit_bytes=8 << 20),
        cost_estimate=pl.CostEstimate(flops=flops, bytes_accessed=1 << 19, transcendentals=0),
    )(*operands)


def pairs(bit):
    return [(s, s | 1 << bit) for s in range(SLOTS) if not s >> bit & 1]


def store(out, nodes, weights):
    rank = nodes[0].shape[0]
    for at, node in enumerate(nodes):
        out[at * rank : (at + 1) * rank] = node
    if weights is not None:
        out[len(nodes) * rank :] = weights


def head_kernel(
    vectors_in,
    basis_in,
    transfer_in,
    target_in,
    diagonal_in,
    out,
    basis,
    target,
    diagonal,
    transfer,
    vectors,
    sems,
):
    leaf = basis.shape[2]
    copies = []

    def fetch(source, to):
        copies.append(pltpu.make_async_copy(source, to, sems.at[len(copies)]))
        copies[-1].start()
        return copies[-1]

    slots = []
    for s in range(SLOTS):
        rows = pl.ds(s * leaf, leaf)
        slots.append(
            (fetch(basis_in.at[s], basis.at[s]), fetch(vectors_in.at[rows], vectors.at[rows]))
        )
    first = fetch(transfer_in.at[pl.ds(0, SLOT_BITS)], transfer)
    weights = fetch(diagonal_in, diagonal)
    later = fetch(target_in, target)
    c = []
    for s in range(SLOTS):
        for copy in slots[s]:
            copy.wait()
        c.append(product(basis[s], vectors[s * leaf : (s + 1) * leaf], NN))
    first.wait()
    for level in range(SLOT_BITS):
        for low, high in pairs(level):
            both = jnp.concatenate([c[low], c[high]], axis=0)
            c[low] = product(transfer[level, low], both, NN)
            c[high] = product(transfer[level, high], both, NN)
    weights.wait()
    store(out, c, diagonal[...])
    later.wait()


def join(level, bit, s, at, own, partner, transfer):
    rank = transfer.shape[2]
    rows = pl.ds(pl.multiple_of(at * rank, rank), rank)
    upper = is_upper(bit)
    lower_half = jnp.where(upper, partner[rows], own[rows])
    upper_half = jnp.where(upper, own[rows], partner[rows])
    return product(transfer[level, s], jnp.concatenate([lower_half, upper_half], axis=0), NN)


def weights_of(bit, own, partner, rank):
    return (partner if bit == 0 else own)[SLOTS * rank :]


def pair_kernel(level, bit, own, partner, transfer, out):
    nodes = [join(level, bit, s, s, own, partner, transfer) for s in range(SLOTS)]
    store(out, nodes, weights_of(bit, own, partner, transfer.shape[2]))


def cutting_pair_kernel(level, bit, own, partner, transfer, *outs):
    for j, piece in enumerate(FORWARD_PIECES):
        nodes = [join(level, bit, met(k), met(k), own, partner, transfer) for k in piece]
        weights = weights_of(bit, own, partner, transfer.shape[2]) if j == 0 else None
        store(outs[j], nodes, weights)


def last_pair_kernel(level, bit, piece, own, partner, transfer, *outs):
    for at, k in enumerate(piece):
        outs[at][...] = join(level, bit, met(k), at, own, partner, transfer)


def weights_kernel(bit, rows, diagonal, partner, out):
    same = bit_of_place(0) == bit_of_place(bit)
    out[...] = jnp.where(same, diagonal[...], partner[rows:])


def tops_of(transfer, levels, s):
    return jnp.concatenate([transfer[level, s] for level in levels], axis=0)


def first_step(read, out):
    x, _ = top_pair()
    for v in range(2):
        out[v] = read((x ^ 1) << 1 | v)


def second_step(read, first, out):
    x, y = top_pair()
    out[x] = read(x << 1 | (y ^ 1))
    out[x ^ 1] = first[y ^ 1]


def settle(read, first, second, write):
    x, y = top_pair()
    write(x << 1 | y, read(x << 1 | y))
    write((x ^ 1) << 1 | y, first[y])
    for w in range(2):
        write(w << 1 | (y ^ 1), second[w])


def basis_first_kernel(basis, out):
    first_step(lambda s: basis[s], out)


def basis_second_kernel(basis, first, out):
    second_step(lambda s: basis[s], first, out)


def basis_settle_kernel(basis, first, second, out):
    def write(s, block):
        out[s] = block

    settle(lambda s: basis[s], first, second, write)


def tops_first_kernel(levels, transfer, out):
    first_step(lambda s: tops_of(transfer, levels, s), out)


def tops_second_kernel(levels, transfer, first, out):
    second_step(lambda s: tops_of(transfer, levels, s), first, out)


def compose(levels, bits, rank):
    blocks = [levels[0, s] for s in range(SLOTS)]
    sources = [[s & ~(1 << bits[0]), s | 1 << bits[0]] for s in range(SLOTS)]
    for j in range(1, SLOT_BITS):
        bit = 1 << bits[j]
        old, old_sources = blocks, sources
        blocks, sources = [], []
        for s in range(SLOTS):
            halves = [
                product(levels[j, s][:, e * rank : (e + 1) * rank], old[q], NN)
                for e, q in enumerate((s & ~bit, s | bit))
            ]
            blocks.append(jnp.concatenate(halves, axis=1))
            sources.append(old_sources[s & ~bit] + old_sources[s | bit])
    return blocks, sources


def fold_kernel(levels, transfer, first, second, basis, weights, wide, middle, tops, columns):
    rank = basis.shape[1]

    def write(s, block):
        for j in range(SLOT_BITS):
            tops[j, s] = block[j * rank : (j + 1) * rank]

    settle(lambda s: tops_of(transfer, levels, s), first, second, write)
    blocks, sources = compose(tops, list(reversed(range(SLOT_BITS))), rank)
    for s in range(SLOTS):
        for at, source in enumerate(sources[s]):
            columns[source, s * rank : (s + 1) * rank] = blocks[s][:, at * rank : (at + 1) * rank]
    ordered = jnp.concatenate([columns[met(k)] for k in range(SLOTS)], axis=1)
    wide[...] = ordered
    inner = []
    for s in range(SLOTS):
        rows = weights.shape[0] // SLOTS
        weight = jnp.concatenate([weights[j : j + 1] for j in range(s * rows, (s + 1) * rows)], axis=1)
        gram = product(basis[s] * weight, basis[s], NT)
        inner.append(product(gram, ordered[s * rank : (s + 1) * rank], NN))
    middle[...] = product(ordered, jnp.concatenate(inner, axis=0), TN)


def middle_kernel(middle, *refs):
    blocks, outs = refs[:SLOTS], refs[SLOTS:]
    rank = blocks[0].shape[0]
    out = product(middle[...], jnp.concatenate([b[...] for b in blocks], axis=0), NN)
    for k in range(SLOTS):
        outs[k][...] = out[k * rank : (k + 1) * rank]


def top_kernel(wide, *refs):
    blocks, out = refs[:SLOTS], refs[SLOTS]
    rank = blocks[0].shape[0]
    rows = product(wide[...], jnp.concatenate([b[...] for b in blocks], axis=0), NN)
    for s in range(SLOTS):
        out[s] = rows[s * rank : (s + 1) * rank]


def part(level, bit, s, at, block, transfer, sent, kept):
    upper = is_upper(bit)
    out = product(transfer[level, s], block, TN)
    rank = sent.shape[1]
    sent[at] = jnp.where(upper, out[:rank], out[rank:])
    kept[at] = jnp.where(upper, out[rank:], out[:rank])


def first_part_kernel(level, bit, piece, transfer, *refs):
    sent, kept = refs[len(piece) :]
    for at, k in enumerate(piece):
        part(level, bit, met(k), at, refs[at][...], transfer, sent, kept)


def joining_part_kernel(level, bit, transfer, *refs):
    sent, kept = refs[-2:]
    for j, piece in enumerate(BACK_PIECES):
        kept_in, arrived = refs[2 * j : 2 * j + 2]
        for at, k in enumerate(piece):
            s = met(k)
            part(level, bit, s, s, kept_in[at] + arrived[at], transfer, sent, kept)


def part_kernel(level, bit, transfer, kept_in, arrived, sent, kept):
    for s in range(SLOTS):
        part(level, bit, s, s, kept_in[s] + arrived[s], transfer, sent, kept)


def write_rows(rows, out, buffer, sems):
    copies = []
    for s in range(SLOTS):
        leaf = buffer.shape[1]
        buffer[s] = rows(s)
        copies.append(
            pltpu.make_async_copy(buffer.at[s], out.at[pl.ds(s * leaf, leaf)], sems.at[s])
        )
        copies[-1].start()
    for copy in copies:
        copy.wait()


def source_fold_kernel(transfer, basis, high, low):
    rank = basis.shape[1]
    blocks, sources = compose(transfer, list(range(SLOT_BITS)), rank)
    rows = jnp.concatenate(blocks, axis=0)
    for at, source in enumerate(sources[0]):
        through = product(rows[:, at * rank : (at + 1) * rank], basis[source], NN)
        high[source], low[source] = split(through.T)


def tail_kernel(kept, arrived, high, low, out, buffer, sems):
    b = jnp.concatenate([kept[s] + arrived[s] for s in range(SLOTS)], axis=0)
    bh, bl = split(b)

    def dot(x, y):
        return lax.dot_general(x, y, (NN, ((), ())), preferred_element_type=jnp.float32)

    write_rows(
        lambda s: dot(high[s], bh) + (dot(high[s], bl) + dot(low[s], bh)), out, buffer, sems
    )


def image_kernel(basis, coeffs, out, buffer, sems):
    write_rows(lambda s: product(basis[s], coeffs[s], TN), out, buffer, sems)


def body(vectors, diagonal, source_basis, transfer, target_basis):
    slots, leaf, rank = source_basis.shape
    vecs = vectors.shape[-1]
    places = Places(SLOT_BITS)
    pair_bits = list(range(places.low_bits))
    nodes, node = (slots, rank, vecs), (rank, vecs)
    basis_shape = (slots, rank, leaf)
    rows_scratch = [pltpu.VMEM((slots, leaf, vecs), jnp.float32), pltpu.SemaphoreType.DMA((slots,))]
    source_t = jnp.swapaxes(source_basis, 1, 2)
    target_t = jnp.swapaxes(target_basis, 1, 2)
    lanes = transfer.shape[3]
    diagonal_rows = diagonal.reshape(-1, lanes)
    packed = (slots * rank + diagonal_rows.shape[0], vecs)
    coeffs, source_t, target_t, diagonal_rows = call(
        head_kernel,
        [packed, basis_shape, basis_shape, diagonal_rows.shape],
        [
            pltpu.with_memory_space_constraint(x, pltpu.HBM)
            for x in (vectors, source_t, transfer, target_t, diagonal_rows)
        ],
        [HBM] * 5,
        scratch=[
            pltpu.VMEM((SLOT_BITS,) + transfer.shape[1:], jnp.float32),
            pltpu.VMEM(vectors.shape, jnp.float32),
            pltpu.SemaphoreType.DMA((2 * slots + 3,)),
        ],
    )
    tops = [SLOT_BITS + places.low_bits + j for j in range(SLOT_BITS)]

    half = (slots // 2, rank, leaf)
    (sent,) = call(basis_first_kernel, [half], [target_t])
    first = places.flip_top(sent, 0)
    (sent,) = call(basis_second_kernel, [half], [target_t, first])
    second = places.flip_top(sent, 1)
    (basis_t,) = call(basis_settle_kernel, [basis_shape], [target_t, first, second])
    image_basis = places.reverse_low(basis_t)
    half = (slots // 2, SLOT_BITS * rank, lanes)
    (sent,) = call(functools.partial(tops_first_kernel, tops), [half], [transfer])
    first = places.flip_top(sent, 0)
    (sent,) = call(functools.partial(tops_second_kernel, tops), [half], [transfer, first])
    second = places.flip_top(sent, 1)

    *early_bits, last_bit = pair_bits
    weight_rows = diagonal_rows.shape[0]
    for bit in early_bits:
        partner = places.partner(coeffs, bit)
        cut = bit == early_bits[-1]
        rows = [len(piece) * rank for piece in FORWARD_PIECES]
        rows[0] += weight_rows
        coeffs, *others = call(
            functools.partial(cutting_pair_kernel if cut else pair_kernel, SLOT_BITS + bit, bit),
            [(n, vecs) for n in rows] if cut else [packed],
            [coeffs, partner, transfer],
        )
    messages = [coeffs] + others
    partners = [places.partner(message, last_bit) for message in messages]
    blocks = {}
    for j, piece in enumerate(FORWARD_PIECES):
        outs = call(
            functools.partial(last_pair_kernel, SLOT_BITS + last_bit, last_bit, piece),
            [node] * len(piece),
            [messages[j], partners[j], transfer],
        )
        blocks.update(zip(piece, outs))
    blocks = [blocks[k] for k in range(SLOTS)]
    if places.low_bits // 2 == 1:
        (weights,) = call(
            functools.partial(weights_kernel, last_bit, len(FORWARD_PIECES[0]) * rank),
            [diagonal_rows.shape],
            [diagonal_rows, partners[0]],
        )
    else:
        weights = places.reverse_low(diagonal).reshape(diagonal_rows.shape)

    square = (slots * rank, slots * rank)
    wide, middle = call(
        functools.partial(fold_kernel, tops),
        [square, square],
        [transfer, first, second, basis_t, weights],
        scratch=[
            pltpu.VMEM((SLOT_BITS, slots, rank, lanes), jnp.float32),
            pltpu.VMEM((slots, slots * rank, rank), jnp.float32),
        ],
    )

    blocks = places.across(blocks)
    back = places.across(call(middle_kernel, [node] * slots, [middle] + blocks))
    (coeffs,) = call(top_kernel, [nodes], [wide] + blocks)
    image_coeffs = places.reverse_low(coeffs)
    (forward_image,) = call(
        image_kernel,
        [vectors.shape],
        [image_basis, image_coeffs],
        out_specs=[ANY],
        scratch=rows_scratch,
    )

    source_fold = call(
        source_fold_kernel,
        [(slots, leaf, slots * rank)] * 2,
        [transfer, source_t],
        kind=jnp.bfloat16,
    )
    pieces = []
    for piece in BACK_PIECES:
        shape = (len(piece), rank, vecs)
        sent, kept = call(
            functools.partial(first_part_kernel, SLOT_BITS + last_bit, last_bit, piece),
            [shape, shape],
            [transfer] + [back[k] for k in piece],
        )
        pieces += [kept, places.partner(sent, last_bit)]
    for bit in reversed(early_bits):
        sent, kept = call(
            functools.partial(
                joining_part_kernel if bit == early_bits[-1] else part_kernel, SLOT_BITS + bit, bit
            ),
            [nodes, nodes],
            [transfer] + pieces,
        )
        pieces = [kept, places.partner(sent, bit)]
    kept, arrived = pieces
    (adjoint,) = call(
        tail_kernel,
        [vectors.shape],
        [kept, arrived, *source_fold],
        out_specs=[ANY],
        scratch=rows_scratch,
    )
    return forward_image, adjoint


def solution(mesh):
    placed = (
        P(BOTH, None),
        P(BOTH),
        P(BOTH, None, None),
        P(None, BOTH, None, None),
        P(BOTH, None, None),
    )

    return jax.shard_map(
        body, mesh=mesh, in_specs=placed, out_specs=(P(BOTH, None), P(BOTH, None)), check_vma=False
    )
```
